32 devices in a mesh: strip: 4 (over z), mr: 8 (over y, x, core).
Axes of the slice: x: 2, y: 2, z: 4, core: 2. Of those that a mesh axis runs over, the one named last changes fastest.
Arguments:
- alm: bfloat16 [2, 256, 2048], P(None, ('strip', 'mr')), may hold values from -6 to 6
- beam: float32 [13, 2048], replicated, may hold values from -6 to 6
- wigner: bfloat16 [256, 13, 32, 2048], P(('strip', 'mr')), may hold values from -0.125 to 0.125
- base_index: int32 [8192], P(('strip', 'mr')), may hold values from 0 to 16124
- interp_weights: float32 [12, 8192], P(None, ('strip', 'mr')), may hold values from -3 to 3
- live_counts: int32 [32, 32], P(('strip', 'mr')), may hold values from 0 to 8, as said below
Outputs:
- tod: float32 [8192], P(('strip', 'mr'))
The draws below stay inside these ranges and needn't reach their ends.
Inputs may be any that keep to these rules, and one draw needn't show every extreme that they name: live_counts[i, d] counts the used slots from device i to block d; blocks differ in how many samples point into them, and some pair uses all 8 slots in every draw.
All inputs are finite; a program needn't handle non-finite values.
Results may differ from the reference program's by a relative error of at most 0.0055.
Values may be sent and summed in bfloat16 or wider, within the bound.
No kernel may reach another device: no remote copies, remote signals or barrier semaphores. Data moves between devices by JAX's collectives and lax.ppermute only.
A program may use at most 64 MiB of HBM per device.

```python
import math
import jax
import jax.numpy as jnp
from jax import lax

ELLS = 2048
ORDERS = 13
LAT_DEV = 4
CAP = 8
M_TOTAL = 256
LATS = 32
PHIS = 512
PHI_DEV = 128
PSIS = 25
SLOTS = 8192
N_MR = 8
DEVICES = 32


def draw_live_counts(key, part):
    key_level = jax.random.fold_in(key, 11)
    key_raw = jax.random.fold_in(key, 12)
    key_src = jax.random.fold_in(key, 13)
    key_dst = jax.random.fold_in(key, 14)
    level = jnp.left_shift(jnp.int32(1), jax.random.randint(key_level, (DEVICES,), 0, 4))
    raw = jax.random.randint(key_raw, (DEVICES, DEVICES), 0, CAP + 1)
    counts = jnp.minimum(CAP, raw * level[None, :] // 4)
    src = jax.random.randint(key_src, (), 0, DEVICES)
    dst = jax.random.randint(key_dst, (), 0, DEVICES)
    return counts.at[src, dst].set(CAP).astype(jnp.int32)


def draw_base_index(key, part):
    key_spread = jax.random.fold_in(key, 21)
    key_pick = jax.random.fold_in(key, 22)
    key_side = jax.random.fold_in(key, 23)
    key_lat = jax.random.fold_in(key, 24)
    key_psi = jax.random.fold_in(key, 25)
    spread_phi = jax.random.randint(key_spread, (SLOTS,), 0, PHI_DEV + 1)
    pick = jax.random.randint(key_pick, (SLOTS,), 0, 4)
    border_phi = jnp.where(pick < 2, pick, PHI_DEV - 3 + pick)
    side = jax.random.randint(key_side, (SLOTS,), 0, 2)
    phi_base = jnp.where(side == 1, border_phi, spread_phi)
    lat_base = jax.random.randint(key_lat, (SLOTS,), 0, LAT_DEV + 1)
    psi_base = jax.random.randint(key_psi, (SLOTS,), 0, PSIS)
    return ((psi_base * (LAT_DEV + 1) + lat_base) * (PHI_DEV + 1) + phi_base).astype(jnp.int32)


def steps_of(stream_key, dims, pieces, smallest, top_value):
    gain, own = 1.0, jax.random.fold_in(stream_key, 6)
    for position, parts in pieces:
        steps = jnp.exp(jax.random.uniform(jax.random.fold_in(own, position), (parts,), jnp.float32, smallest / len(pieces), top_value / len(pieces)))
        gain = gain * jnp.repeat(steps, dims[position] // parts).reshape([-1 if axis == position else 1 for axis in range(len(dims))])
    return gain


def noise(own_key, extent, width, bound, split=(), held_as=jnp.bfloat16):
    entries = width * jax.random.normal(own_key, extent, jnp.float32)
    if split:
        entries = entries * steps_of(own_key, extent, split, -0.22, 0.18)
    return jnp.clip(entries, -bound, bound).astype(held_as)


def setup_inputs(seed: int = 0) -> dict:
    keys = jax.random.split(jax.random.key(seed), 7)
    return {
        "alm": noise(keys[0], (2, M_TOTAL, ELLS), 1.0, 6.0, ((1, 32),)),
        "beam": noise(keys[1], (ORDERS, ELLS), 1.0, 6.0, (), jnp.float32),
        "wigner": noise(keys[2], (M_TOTAL, ORDERS, LATS, ELLS), ELLS ** -0.5, 0.125, ((0, 32),)),
        "base_index": draw_base_index(jax.random.fold_in(keys[6], 71), 0),
        "interp_weights": noise(keys[4], (12, SLOTS), 0.5, 3.0, ((1, 32),), jnp.float32),
        "live_counts": draw_live_counts(jax.random.fold_in(keys[6], 71), 0),
    }


def phase_tables(m_first, m_count, phi_first, phi_count, phi_total):
    m_vals = m_first + jnp.arange(m_count, dtype=jnp.int32)
    phi_vals = phi_first + jnp.arange(phi_count, dtype=jnp.int32)
    product = phi_vals[:, None] * m_vals[None, :] % phi_total
    angle = 2.0 * math.pi / phi_total * product.astype(jnp.float32)
    return (jnp.cos(angle).astype(jnp.bfloat16), jnp.sin(angle).astype(jnp.bfloat16))

def orient_table(psi_count, k_count):
    product = jnp.arange(psi_count, dtype=jnp.int32)[:, None] * jnp.arange(k_count, dtype=jnp.int32)[None, :] % psi_count
    angle = 2.0 * math.pi / psi_count * product.astype(jnp.float32)
    return jnp.stack([jnp.cos(angle), -jnp.sin(angle)], axis=1)

def reference(alm, beam, wigner, base_index, interp_weights, live_counts):
    mixed = (alm[:, :, None, :].astype(jnp.float32) * beam[None, None, :, :]).astype(jnp.bfloat16)

    def per_order(items):
        mixed_m, table_m = items
        return jnp.einsum('ckl,krl->ckr', mixed_m.astype(jnp.float32), table_m.astype(jnp.float32), precision=lax.Precision.HIGHEST)
    coef = lax.map(per_order, (jnp.moveaxis(mixed, 1, 0), wigner))
    coef = jnp.moveaxis(coef, 0, 1).astype(jnp.bfloat16).reshape(2, M_TOTAL, ORDERS * LATS)
    cos_table, sin_table = phase_tables(0, M_TOTAL, 0, PHIS, PHIS)
    real_part = jnp.dot(cos_table, coef[0], preferred_element_type=jnp.float32) - jnp.dot(sin_table, coef[1], preferred_element_type=jnp.float32)
    imag_part = jnp.dot(sin_table, coef[0], preferred_element_type=jnp.float32) + jnp.dot(cos_table, coef[1], preferred_element_type=jnp.float32)
    spectra = jnp.stack([real_part.reshape(PHIS, ORDERS, LATS), imag_part.reshape(PHIS, ORDERS, LATS)], axis=1)
    scale = 1.0 / math.sqrt(M_TOTAL * ORDERS)
    cube = (jnp.einsum('pckr,tck->trp', spectra, orient_table(PSIS, ORDERS), precision=lax.Precision.HIGHEST) * scale).astype(jnp.bfloat16)
    bases = base_index.reshape(DEVICES, DEVICES, CAP)
    weights = jnp.moveaxis(interp_weights.reshape(12, DEVICES, DEVICES, CAP), 1, 0)

    def per_source(items):
        base, wts, counts = items
        dest = jnp.arange(DEVICES, dtype=jnp.int32)[:, None]
        strip_of = dest // N_MR
        mr_of = dest % N_MR
        phi_base = base % (PHI_DEV + 1)
        rest = base // (PHI_DEV + 1)
        lat_base = rest % (LAT_DEV + 1)
        psi_base = rest // (LAT_DEV + 1)
        offs = jnp.arange(4, dtype=jnp.int32)[:, None, None]
        psi_idx = (psi_base[None] + offs) % PSIS
        lat_idx = (mr_of * LAT_DEV + lat_base - 2 + offs) % LATS
        phi_idx = (strip_of * PHI_DEV + phi_base - 2 + offs) % PHIS
        values = cube[psi_idx[:, None, None], lat_idx[None, :, None], phi_idx[None, None, :]].astype(jnp.float32)
        live = (jnp.arange(CAP, dtype=jnp.int32)[None, :] < counts[:, None]).astype(jnp.float32)
        lat_w = wts[0:4] * live[None]
        prod = values * wts[8:12][:, None, None] * lat_w[None, :, None] * wts[4:8][None, None, :]
        return lax.optimization_barrier(jnp.sum(prod, axis=(0, 1, 2)))
    result = lax.map(per_source, (bases, weights, live_counts))
    return result.reshape(SLOTS)
```

```python
import functools
import math

import jax
import jax.numpy as jnp
import numpy as np
from jax import lax
from jax.experimental import pallas as pl
from jax.experimental.pallas import tpu as pltpu
from jax.sharding import PartitionSpec as P

NT = (((1,), (1,)), ((), ()))
VMEM = pl.BlockSpec(memory_space=pltpu.VMEM)


def coef_kernel(alm_hbm, beam_hbm, table_hbm, out_ref, alm, beam, table, mixed, rows, sems):
    orders, beam_rows, ells = table.shape
    k_count = beam.shape[0]
    lats = beam_rows // k_count
    k_pad = mixed.shape[1] // 2
    small = [
        pltpu.make_async_copy(alm_hbm, alm, sems.at[orders]),
        pltpu.make_async_copy(beam_hbm, beam, sems.at[orders + 1]),
    ]
    big = [
        pltpu.make_async_copy(table_hbm.at[m], table.at[m], sems.at[m]) for m in range(orders)
    ]
    for copy in small + big:
        copy.start()
    mixed[...] = jnp.zeros_like(mixed)
    for copy in small:
        copy.wait()
    for m in range(orders):
        for c in range(2):
            product = alm[c, m, :].astype(jnp.float32)[None, :] * beam[...]
            mixed[m, c * k_pad : c * k_pad + k_count, :] = product.astype(jnp.bfloat16)
    for m in range(orders):
        big[m].wait()
        y = lax.dot_general(mixed[m], table[m], NT, preferred_element_type=jnp.float32)
        of_row = lax.broadcasted_iota(jnp.int32, y.shape, 0) % k_pad
        of_lane = lax.broadcasted_iota(jnp.int32, y.shape, 1) // lats
        y = jnp.where(of_row == of_lane, y, 0.0)
        for c in range(2):
            total = jnp.sum(y[c * k_pad : (c + 1) * k_pad], axis=0, keepdims=True)
            rows[c * orders + m : c * orders + m + 1, :] = total
    out_ref[...] = rows[...].astype(jnp.bfloat16)


def local_coef(alm, beam, wigner):
    orders, k_count, lats, ells = wigner.shape
    k_pad = -(-k_count // 8) * 8
    anywhere = pl.BlockSpec(memory_space=pl.ANY)
    return pl.pallas_call(
        coef_kernel,
        out_shape=jax.ShapeDtypeStruct((2 * orders, k_count * lats), jnp.bfloat16),
        in_specs=[anywhere] * 3,
        out_specs=VMEM,
        scratch_shapes=[
            pltpu.VMEM((2, orders, ells), jnp.bfloat16),
            pltpu.VMEM((k_count, ells), jnp.float32),
            pltpu.VMEM((orders, k_count * lats, ells), jnp.bfloat16),
            pltpu.VMEM((orders, 2 * k_pad, ells), jnp.bfloat16),
            pltpu.VMEM((2 * orders, k_count * lats), jnp.float32),
            pltpu.SemaphoreType.DMA((orders + 2,)),
        ],
        compiler_params=pltpu.CompilerParams(vmem_limit_bytes=40 << 20),
        cost_estimate=pl.CostEstimate(
            flops=4 * wigner.size, bytes_accessed=2 * wigner.size, transcendentals=0
        ),
        name="coef",
    )(alm, beam, wigner.reshape(orders, k_count * lats, ells))


def cos_sin_turns(x):
    x = x - jnp.round(x)
    u = x * x
    cos = jnp.zeros_like(x)
    sin = jnp.zeros_like(x)
    for n in range(9, -1, -1):
        cos = cos * u + (-1) ** n * (2 * math.pi) ** (2 * n) / math.factorial(2 * n)
        sin = sin * u + (-1) ** n * (2 * math.pi) ** (2 * n + 1) / math.factorial(2 * n + 1)
    return cos, sin * x


def remainder(x, n):
    return x - n * jnp.floor((x + 0.5) * (1.0 / n))


def weights_kernel(
    sizes, slots_ref, counts_ref, order_ref, lane_ref, re_ref, im_ref, tail_re_ref, tail_im_ref
):
    cap, phi_total, lats, psi_count, lat_dev, phi_dev, scale = sizes
    cols = slots_ref[...].T
    count = cols.shape[0]
    base, slot_e, strip_phi, mr_lat = (cols[:, i : i + 1] for i in range(12, 16))
    dest = lax.broadcasted_iota(jnp.int32, (count, counts_ref.shape[1]), 1).astype(jnp.float32)
    of_slot = cols[:, 16:17]
    used = jnp.sum(
        jnp.where(dest == of_slot, counts_ref[...].astype(jnp.float32), 0.0), axis=1, keepdims=True
    )
    live = (slot_e < used).astype(jnp.float32)
    rest = jnp.floor((base + 0.5) * (1.0 / (phi_dev + 1)))
    phi_base = base - rest * (phi_dev + 1)
    psi_base = jnp.floor((rest + 0.5) * (1.0 / (lat_dev + 1)))
    lat_base = rest - psi_base * (lat_dev + 1)

    order, quarter = order_ref[0:1], order_ref[1:2]
    cos, sin = cos_sin_turns((strip_phi + phi_base - 2.0) * order * (1.0 / phi_total) + quarter)
    sum_re = cols[:, 4:5] * jnp.ones_like(order)
    sum_im = jnp.zeros_like(sum_re)
    for b in range(1, 4):
        step_cos, step_sin = cos_sin_turns(b * order * (1.0 / phi_total))
        sum_re = sum_re + cols[:, 4 + b : 5 + b] * step_cos
        sum_im = sum_im + cols[:, 4 + b : 5 + b] * step_sin
    re_ref[...] = (cos * sum_re - sin * sum_im).astype(jnp.bfloat16)
    im_ref[...] = (sin * sum_re + cos * sum_im).astype(jnp.bfloat16)

    k_lane, r_lane = lane_ref[0:1], lane_ref[1:2]
    cos, sin = cos_sin_turns(remainder(psi_base * k_lane, psi_count) * (1.0 / psi_count))
    sum_re = cols[:, 8:9] * jnp.ones_like(k_lane)
    sum_im = jnp.zeros_like(sum_re)
    for c in range(1, 4):
        step_cos, step_sin = cos_sin_turns(remainder(c * k_lane, psi_count) * (1.0 / psi_count))
        sum_re = sum_re + cols[:, 8 + c : 9 + c] * step_cos
        sum_im = sum_im + cols[:, 8 + c : 9 + c] * step_sin
    across = jnp.zeros_like(sum_re)
    for a in range(4):
        row = remainder(mr_lat + lat_base - 2.0 + a, lats)
        across = across + jnp.where(row == r_lane, cols[:, a : a + 1] * live, 0.0)
    across = across * scale
    tail_re_ref[...] = (cos * sum_re - sin * sum_im) * across
    tail_im_ref[...] = -(sin * sum_re + cos * sum_im) * across


def sample_weights(base_index, interp_weights, live_counts, order, quarter, sizes, n_mr, k_count):
    cap, phi_total, lats, psi_count, lat_dev, phi_dev, scale = sizes
    slots = base_index.shape[0]
    dest = np.arange(slots) // cap
    fixed = np.zeros((19, slots), np.float32)
    fixed[0] = np.arange(slots) % cap
    fixed[1] = dest // n_mr * phi_dev
    fixed[2] = dest % n_mr * lat_dev
    fixed[3] = dest
    table = jnp.concatenate(
        [interp_weights, base_index[None].astype(jnp.float32), jnp.asarray(fixed)], axis=0
    )
    lane = np.zeros((8, k_count * lats), np.float32)
    lane[0] = np.arange(k_count * lats) // lats
    lane[1] = np.arange(k_count * lats) % lats
    orders = jnp.stack([order, quarter] + [jnp.zeros_like(order)] * 6)
    block = min(slots, 256)
    width = order.shape[0]
    lanes = k_count * lats
    whole = lambda shape: pl.BlockSpec(shape, lambda i: (0, 0))
    return pl.pallas_call(
        functools.partial(weights_kernel, sizes),
        grid=(slots // block,),
        out_shape=(
            jax.ShapeDtypeStruct((slots, width), jnp.bfloat16),
            jax.ShapeDtypeStruct((slots, width), jnp.bfloat16),
            jax.ShapeDtypeStruct((slots, lanes), jnp.float32),
            jax.ShapeDtypeStruct((slots, lanes), jnp.float32),
        ),
        in_specs=[
            pl.BlockSpec((32, block), lambda i: (0, i)),
            whole(live_counts.shape),
            whole(orders.shape),
            whole(lane.shape),
        ],
        out_specs=(
            pl.BlockSpec((block, width), lambda i: (i, 0)),
            pl.BlockSpec((block, width), lambda i: (i, 0)),
            pl.BlockSpec((block, lanes), lambda i: (i, 0)),
            pl.BlockSpec((block, lanes), lambda i: (i, 0)),
        ),
        compiler_params=pltpu.CompilerParams(vmem_limit_bytes=32 << 20),
        cost_estimate=pl.CostEstimate(
            flops=60 * slots * (width + lanes), bytes_accessed=1 << 20, transcendentals=0
        ),
        name="weights",
    )(table, live_counts, orders, jnp.asarray(lane))


def sample_kernel(re_ref, im_ref, tail_re_ref, tail_im_ref, *refs):
    parts, out_ref, coef = refs[:-2], refs[-2], refs[-1]
    start = 0
    for part in parts:
        coef[start : start + part.shape[0], :] = part[...]
        start += part.shape[0]
    real = jnp.dot(re_ref[...], coef[...], preferred_element_type=jnp.float32)
    imag = jnp.dot(im_ref[...], coef[...], preferred_element_type=jnp.float32)
    terms = real * tail_re_ref[...] + imag * tail_im_ref[...]
    out_ref[...] = jnp.sum(terms.T, axis=0, keepdims=True)


def sample(phases, parts):
    slots, width = phases[0].shape
    lanes = phases[2].shape[1]
    block = min(slots, 256)
    rows = lambda n: pl.BlockSpec((block, n), lambda i: (i, 0))
    return pl.pallas_call(
        sample_kernel,
        grid=(slots // block,),
        out_shape=jax.ShapeDtypeStruct((1, slots), jnp.float32),
        in_specs=[rows(width), rows(width), rows(lanes), rows(lanes)]
        + [pl.BlockSpec(part.shape, lambda i: (0, 0)) for part in parts],
        out_specs=pl.BlockSpec((1, block), lambda i: (0, i)),
        scratch_shapes=[pltpu.VMEM((width, lanes), jnp.bfloat16)],
        compiler_params=pltpu.CompilerParams(vmem_limit_bytes=32 << 20),
        cost_estimate=pl.CostEstimate(
            flops=4 * slots * width * lanes, bytes_accessed=1 << 20, transcendentals=0
        ),
        name="sample",
    )(*phases, *parts)


def on_device(alm, beam, wigner, base_index, interp_weights, live_counts):
    n_strip = lax.axis_size("strip")
    n_mr = lax.axis_size("mr")
    devices = n_strip * n_mr
    orders, k_count, lats, _ = wigner.shape
    m_total = orders * devices
    phi_total = 2 * m_total
    psi_count = 2 * k_count - 1
    sizes = (
        base_index.shape[0] // devices,
        phi_total,
        lats,
        psi_count,
        lats // n_mr,
        phi_total // n_strip,
        1.0 / math.sqrt(m_total * k_count),
    )
    chips = n_mr // 2
    strip_at = lax.axis_index("strip")
    mr_at = lax.axis_index("mr")

    shape = (2, chips, n_strip, 2, orders)
    index = lambda axis: lax.broadcasted_iota(jnp.int32, shape, axis)
    from_strip = (strip_at - index(2)) % n_strip
    from_mr = 2 * ((mr_at // 2 - index(1)) % chips) + (mr_at % 2 + index(0)) % 2
    order = (from_strip * n_mr + from_mr) * orders + index(4)
    order = order.reshape(-1).astype(jnp.float32)
    quarter = (0.25 * index(3)).reshape(-1).astype(jnp.float32)
    phases = sample_weights(
        base_index, interp_weights, live_counts, order, quarter, sizes, n_mr, k_count
    )

    mine = local_coef(alm, beam, wigner)
    column = [mine] + [
        lax.ppermute(mine, "strip", [(i, (i + d) % n_strip) for i in range(n_strip)])
        for d in range(1, n_strip)
    ]
    column = jnp.concatenate(column, axis=0)
    plane = [column] + [
        lax.ppermute(column, "mr", [(i, (i + 2 * d) % n_mr) for i in range(n_mr)])
        for d in range(1, chips)
    ]
    other = [lax.ppermute(part, "mr", [(i, i ^ 1) for i in range(n_mr)]) for part in plane]
    return sample(phases, plane + other).reshape(-1)


def solution(mesh):
    placed = (
        P(None, ("strip", "mr"), None),
        P(),
        P(("strip", "mr"), None, None, None),
        P(("strip", "mr")),
        P(None, ("strip", "mr")),
        P(("strip", "mr"), None),
    )
    return jax.shard_map(
        on_device, mesh=mesh, in_specs=placed, out_specs=P(("strip", "mr")), check_vma=False
    )
```

```python
import functools
import math

import jax
import jax.numpy as jnp
import numpy as np
from jax import lax
from jax.experimental import pallas as pl
from jax.experimental.pallas import tpu as pltpu
from jax.sharding import PartitionSpec as P

NT = (((1,), (1,)), ((), ()))
VMEM = pl.BlockSpec(memory_space=pltpu.VMEM)


def cos_sin_turns(x):
    x = x - jnp.round(x)
    u = x * x
    cos = jnp.zeros_like(x)
    sin = jnp.zeros_like(x)
    for n in range(9, -1, -1):
        cos = cos * u + (-1) ** n * (2 * math.pi) ** (2 * n) / math.factorial(2 * n)
        sin = sin * u + (-1) ** n * (2 * math.pi) ** (2 * n + 1) / math.factorial(2 * n + 1)
    return cos, sin * x


def remainder(x, n):
    return x - n * jnp.floor((x + 0.5) * (1.0 / n))


def tap_phases(taps, turns):
    total_re = taps[0] * jnp.ones_like(turns)
    total_im = jnp.zeros_like(total_re)
    for tap in range(1, 4):
        cos, sin = cos_sin_turns(tap * turns)
        total_re = total_re + taps[tap] * cos
        total_im = total_im + taps[tap] * sin
    return total_re, total_im


def turned(turns, values):
    cos, sin = cos_sin_turns(turns)
    return cos * values[0] - sin * values[1], sin * values[0] + cos * values[1]


def slot_weights(sizes, cols, counts, order, quarter, k_lane, r_lane):
    phi_total, lats, psi_count, lat_dev, phi_dev, scale = sizes
    col = lambda i: cols[:, i : i + 1]
    base, slot_e, strip_phi, mr_lat, of_slot = (col(i) for i in range(12, 17))
    dest = lax.broadcasted_iota(jnp.int32, (cols.shape[0], counts.shape[1]), 1)
    used = jnp.where(dest.astype(jnp.float32) == of_slot, counts, 0.0)
    live = (slot_e < jnp.sum(used, axis=1, keepdims=True)).astype(jnp.float32)
    rest = jnp.floor((base + 0.5) * (1.0 / (phi_dev + 1)))
    phi_base = base - rest * (phi_dev + 1)
    psi_base = jnp.floor((rest + 0.5) * (1.0 / (lat_dev + 1)))
    lat_base = rest - psi_base * (lat_dev + 1)
    phases = turned(
        (strip_phi + phi_base - 2.0) * (order * (1.0 / phi_total)) + quarter,
        tap_phases([col(4 + b) for b in range(4)], order * (1.0 / phi_total)),
    )
    across = jnp.zeros((cols.shape[0], k_lane.shape[1]), jnp.float32)
    for a in range(4):
        row = remainder(mr_lat + lat_base - 2.0 + a, lats)
        across = across + jnp.where(row == r_lane, col(a) * live, 0.0)
    across = across * scale
    tail_re, tail_im = turned(
        remainder(psi_base * k_lane, psi_count) * (1.0 / psi_count),
        tap_phases([col(8 + c) for c in range(4)], k_lane * (1.0 / psi_count)),
    )
    return phases + (tail_re * across, -tail_im * across)


def coef_kernel(
    sizes,
    alm_hbm,
    beam_hbm,
    table_hbm,
    slots_ref,
    counts_ref,
    from_ref,
    lane_ref,
    out_ref,
    re_ref,
    im_ref,
    tail_re_ref,
    tail_im_ref,
    alm,
    beam,
    table,
    mixed,
    rows,
    cols,
    sems,
):
    orders, beam_rows, ells = table.shape
    k_count = beam.shape[0]
    lats = beam_rows // k_count
    k_pad = mixed.shape[1] // 2
    small = [
        pltpu.make_async_copy(alm_hbm, alm, sems.at[orders]),
        pltpu.make_async_copy(beam_hbm, beam, sems.at[orders + 1]),
    ]
    big = [
        pltpu.make_async_copy(table_hbm.at[m], table.at[m], sems.at[m]) for m in range(orders)
    ]
    for copy in small + big:
        copy.start()
    mixed[...] = jnp.zeros_like(mixed)
    cols[...] = slots_ref[...].T
    strip_at, mr_at = lax.axis_index("strip"), lax.axis_index("mr")
    source = (from_ref[0:1] ^ strip_at) * lax.axis_size("mr") + (from_ref[1:2] ^ mr_at)
    order = (source * orders + from_ref[2:3]).astype(jnp.float32)
    quarter = 0.25 * from_ref[3:4].astype(jnp.float32)
    counts = counts_ref[...].astype(jnp.float32)
    block = cols.shape[0] // orders

    def mix(m):
        for c in range(2):
            product = alm[c, m, :].astype(jnp.float32)[None, :] * beam[...]
            mixed[m, c * k_pad : c * k_pad + k_count, :] = product.astype(jnp.bfloat16)

    for copy in small:
        copy.wait()
    mix(0)
    for m in range(orders):
        big[m].wait()
        y = lax.dot_general(mixed[m], table[m], NT, preferred_element_type=jnp.float32)
        of_row = lax.broadcasted_iota(jnp.int32, y.shape, 0) % k_pad
        of_lane = lax.broadcasted_iota(jnp.int32, y.shape, 1) // lats
        y = jnp.where(of_row == of_lane, y, 0.0)
        for c in range(2):
            total = jnp.sum(y[c * k_pad : (c + 1) * k_pad], axis=0, keepdims=True)
            rows[c * orders + m : c * orders + m + 1, :] = total
        here = slice(m * block, (m + 1) * block)
        re, im, tail_re, tail_im = slot_weights(
            sizes, cols[here], counts, order, quarter, lane_ref[0:1], lane_ref[1:2]
        )
        re_ref[here] = re.astype(jnp.bfloat16)
        im_ref[here] = im.astype(jnp.bfloat16)
        tail_re_ref[here] = tail_re
        tail_im_ref[here] = tail_im
        if m + 1 < orders:
            mix(m + 1)
    out_ref[...] = rows[...].astype(jnp.bfloat16)


def local_part(alm, beam, wigner, base_index, interp_weights, live_counts, n_strip, n_mr):
    orders, k_count, lats, ells = wigner.shape
    k_pad = -(-k_count // 8) * 8
    lanes = k_count * lats
    slots = base_index.shape[0]
    devices = n_strip * n_mr
    width = 2 * orders * devices
    m_total = orders * devices
    phi_total = 2 * m_total
    lat_dev, phi_dev = lats // n_mr, phi_total // n_strip
    scale = 1.0 / math.sqrt(m_total * k_count)
    sizes = (phi_total, lats, 2 * k_count - 1, lat_dev, phi_dev, scale)

    dest = np.arange(slots) // (slots // devices)
    fixed = np.zeros((19, slots), np.float32)
    fixed[0] = np.arange(slots) % (slots // devices)
    fixed[1] = dest // n_mr * phi_dev
    fixed[2] = dest % n_mr * lat_dev
    fixed[3] = dest
    table = jnp.concatenate(
        [interp_weights, base_index[None].astype(jnp.float32), jnp.asarray(fixed)], axis=0
    )
    core, chip, strip, part, m = np.indices((2, n_mr // 2, n_strip, 2, orders)).reshape(5, -1)
    source = np.zeros((8, width), np.int32)
    source[:4] = [strip, 2 * chip + core, m, part]
    lane = np.zeros((8, lanes), np.float32)
    lane[0] = np.arange(lanes) // lats
    lane[1] = np.arange(lanes) % lats
    hbm = pl.BlockSpec(memory_space=pltpu.HBM)
    return pl.pallas_call(
        functools.partial(coef_kernel, sizes),
        out_shape=(
            jax.ShapeDtypeStruct((2 * orders, lanes), jnp.bfloat16),
            jax.ShapeDtypeStruct((slots, width), jnp.bfloat16),
            jax.ShapeDtypeStruct((slots, width), jnp.bfloat16),
            jax.ShapeDtypeStruct((slots, lanes), jnp.float32),
            jax.ShapeDtypeStruct((slots, lanes), jnp.float32),
        ),
        in_specs=[hbm] * 3 + [VMEM] * 4,
        out_specs=(VMEM,) * 5,
        scratch_shapes=[
            pltpu.VMEM((2, orders, ells), jnp.bfloat16),
            pltpu.VMEM((k_count, ells), jnp.float32),
            pltpu.VMEM((orders, lanes, ells), jnp.bfloat16),
            pltpu.VMEM((orders, 2 * k_pad, ells), jnp.bfloat16),
            pltpu.VMEM((2 * orders, lanes), jnp.float32),
            pltpu.VMEM((slots, 32), jnp.float32),
            pltpu.SemaphoreType.DMA((orders + 2,)),
        ],
        compiler_params=pltpu.CompilerParams(vmem_limit_bytes=48 << 20),
        cost_estimate=pl.CostEstimate(
            flops=4 * wigner.size, bytes_accessed=2 * wigner.size, transcendentals=0
        ),
        name="coef",
    )(
        alm,
        beam,
        wigner.reshape(orders, lanes, ells),
        table,
        live_counts,
        jnp.asarray(source),
        jnp.asarray(lane),
    )


def sample_kernel(re_ref, im_ref, tail_re_ref, tail_im_ref, *refs):
    parts, out_ref, coef = refs[:-2], refs[-2], refs[-1]
    start = 0
    for part in parts:
        coef[start : start + part.shape[0], :] = part[...]
        start += part.shape[0]
    real = jnp.dot(re_ref[...], coef[...], preferred_element_type=jnp.float32)
    imag = jnp.dot(im_ref[...], coef[...], preferred_element_type=jnp.float32)
    terms = real * tail_re_ref[...] + imag * tail_im_ref[...]
    lanes = terms.shape[1]
    whole = lanes // 128 * 128
    total = jnp.zeros((1, terms.shape[0]), jnp.float32)
    if whole:
        tiles = [terms[:, i : i + 128] for i in range(0, whole, 128)]
        total = total + jnp.sum(sum(tiles).T, axis=0, keepdims=True)
    if whole < lanes:
        total = total + jnp.sum(terms[:, whole:].T, axis=0, keepdims=True)
    out_ref[...] = total


def sample(phases, parts):
    slots, width = phases[0].shape
    lanes = phases[2].shape[1]
    block = min(slots, 256)
    rows = lambda n: pl.BlockSpec((block, n), lambda i: (i, 0))
    return pl.pallas_call(
        sample_kernel,
        grid=(slots // block,),
        out_shape=jax.ShapeDtypeStruct((1, slots), jnp.float32),
        in_specs=[rows(width), rows(width), rows(lanes), rows(lanes)]
        + [pl.BlockSpec(part.shape, lambda i: (0, 0)) for part in parts],
        out_specs=pl.BlockSpec((1, block), lambda i: (0, i)),
        scratch_shapes=[pltpu.VMEM((width, lanes), jnp.bfloat16)],
        compiler_params=pltpu.CompilerParams(vmem_limit_bytes=32 << 20),
        cost_estimate=pl.CostEstimate(
            flops=4 * slots * width * lanes, bytes_accessed=1 << 20, transcendentals=0
        ),
        name="sample",
    )(*phases, *parts)


def on_device(alm, beam, wigner, base_index, interp_weights, live_counts):
    n_strip = lax.axis_size("strip")
    n_mr = lax.axis_size("mr")
    mine, *phases = local_part(
        alm, beam, wigner, base_index, interp_weights, live_counts, n_strip, n_mr
    )

    def swap(x, axis, d):
        return lax.ppermute(x, axis, [(i, i ^ d) for i in range(lax.axis_size(axis))])

    column = [swap(mine, "strip", d) for d in range(n_strip - 1, 0, -1)][::-1]
    column = jnp.concatenate([mine] + column, axis=0)
    plane = [column] + [swap(column, "mr", d) for d in range(n_mr - 2, 0, -2)][::-1]
    other = [swap(part, "mr", 1) for part in plane]
    return sample(phases, plane + other).reshape(-1)


def solution(mesh):
    placed = (
        P(None, ("strip", "mr"), None),
        P(),
        P(("strip", "mr"), None, None, None),
        P(("strip", "mr")),
        P(None, ("strip", "mr")),
        P(("strip", "mr"), None),
    )
    return jax.shard_map(
        on_device, mesh=mesh, in_specs=placed, out_specs=P(("strip", "mr")), check_vma=False
    )
```

```python
import functools
import math

import jax
import jax.numpy as jnp
from jax import lax
from jax.experimental import pallas as pl
from jax.experimental.pallas import tpu as pltpu
from jax.sharding import PartitionSpec as P

NT = (((1,), (1,)), ((), ()))
VMEM = pl.BlockSpec(memory_space=pltpu.VMEM)


def cos_sin_turns(x):
    x = x - jnp.round(x)
    u = x * x
    cos = jnp.zeros_like(x)
    sin = jnp.zeros_like(x)
    for n in range(9, -1, -1):
        cos = cos * u + (-1) ** n * (2 * math.pi) ** (2 * n) / math.factorial(2 * n)
        sin = sin * u + (-1) ** n * (2 * math.pi) ** (2 * n + 1) / math.factorial(2 * n + 1)
    return cos, sin * x


def tap_phases(taps, turns):
    total_re = taps[0] * jnp.ones_like(turns)
    total_im = jnp.zeros_like(total_re)
    for tap in range(1, 4):
        cos, sin = cos_sin_turns(tap * turns)
        total_re = total_re + taps[tap] * cos
        total_im = total_im + taps[tap] * sin
    return total_re, total_im


def turned(turns, values):
    cos, sin = cos_sin_turns(turns)
    return cos * values[0] - sin * values[1], sin * values[0] + cos * values[1]


def divide(x, n):
    quotient = jnp.floor((x + 0.5) * (1.0 / n))
    return quotient, x - n * quotient


def slot_rows(sizes, weights, base, counts, n_strip, n_mr):
    phi_total, lats, psi_count, scale = sizes
    slots = weights.shape[1]
    devices = n_strip * n_mr
    lat_dev, phi_dev = lats // n_mr, phi_total // n_strip
    slot = lax.broadcasted_iota(jnp.int32, (1, slots), 1).astype(jnp.float32)
    dest, at = divide(slot, slots // devices)
    dest_strip, dest_mr = divide(dest, n_mr)
    dests = lax.broadcasted_iota(jnp.int32, (devices, slots), 0).astype(jnp.float32)
    counts = jnp.broadcast_to(counts.astype(jnp.float32), (8, devices)).astype(jnp.bfloat16)
    used = jnp.dot(
        counts, (dests == dest).astype(jnp.bfloat16), preferred_element_type=jnp.float32
    )
    live = (at < used[0:1]).astype(jnp.float32)
    rest, phi_base = divide(base.astype(jnp.float32), phi_dev + 1)
    psi_base, lat_base = divide(rest, lat_dev + 1)
    return jnp.concatenate(
        [
            weights[0:4] * (live * scale),
            weights[4:],
            dest_strip * phi_dev + phi_base - 2.0,
            dest_mr * lat_dev + lat_base - 2.0,
            psi_base,
            jnp.zeros_like(base, jnp.float32),
        ],
        axis=0,
    )


def slot_weights(sizes, cols, order, quarter, k_lane, r_lane):
    phi_total, lats, psi_count, _ = sizes
    col = lambda i: cols[:, i : i + 1]
    turns = order * (1.0 / phi_total)
    phases = turned(col(12) * turns + quarter, tap_phases([col(4 + b) for b in range(4)], turns))
    across = jnp.zeros((cols.shape[0], k_lane.shape[1]), jnp.float32)
    for a in range(4):
        _, row = divide(col(13) + a, lats)
        across = across + jnp.where(row == r_lane, col(a), 0.0)
    tail_re, tail_im = turned(
        divide(col(14) * k_lane, psi_count)[1] * (1.0 / psi_count),
        tap_phases([col(8 + c) for c in range(4)], k_lane * (1.0 / psi_count)),
    )
    return phases + (tail_re * across, -tail_im * across)


def coef_kernel(
    sizes,
    alm_hbm,
    beam_hbm,
    table_hbm,
    weights_hbm,
    base_hbm,
    counts_hbm,
    out_ref,
    re_ref,
    im_ref,
    tail_re_ref,
    tail_im_ref,
    alm,
    beam,
    table,
    weights,
    base,
    counts,
    mixed,
    rows,
    cols,
    sems,
):
    n_strip, n_mr = lax.axis_size("strip"), lax.axis_size("mr")
    orders, lanes, ells = table.shape
    k_count = beam.shape[0]
    lats = lanes // k_count
    k_pad = mixed.shape[1] // 2
    small = [(alm_hbm, alm), (beam_hbm, beam)]
    slot = [(weights_hbm, weights), (base_hbm, base), (counts_hbm, counts)]
    pairs = small + slot + [(table_hbm.at[m], table.at[m]) for m in range(orders)]
    copies = [
        pltpu.make_async_copy(source, target, sems.at[i])
        for i, (source, target) in enumerate(pairs)
    ]
    small, slot, big = copies[:2], copies[2:5], copies[5:]
    for copy in copies:
        copy.start()
    mixed[...] = jnp.zeros_like(mixed)

    width = re_ref.shape[1]
    at = lax.broadcasted_iota(jnp.int32, (1, width), 1).astype(jnp.float32)
    at, m_row = divide(at, orders)
    at, part = divide(at, 2)
    at, strip = divide(at, n_strip)
    core, chip = divide(at, n_mr // 2)
    strip = strip.astype(jnp.int32) ^ lax.axis_index("strip")
    mr = (2.0 * chip + core).astype(jnp.int32) ^ lax.axis_index("mr")
    order = ((strip * n_mr + mr) * orders).astype(jnp.float32) + m_row
    quarter = 0.25 * part
    lane = lax.broadcasted_iota(jnp.int32, (1, lanes), 1).astype(jnp.float32)
    k_lane, r_lane = divide(lane, lats)

    for copy in slot:
        copy.wait()
    cols[...] = slot_rows(sizes, weights[...], base[...], counts[...], n_strip, n_mr).T
    block = cols.shape[0] // orders

    def mix(m):
        for c in range(2):
            product = alm[c, m, :].astype(jnp.float32)[None, :] * beam[...]
            mixed[m, c * k_pad : c * k_pad + k_count, :] = product.astype(jnp.bfloat16)

    for copy in small:
        copy.wait()
    mix(0)
    for m in range(orders):
        big[m].wait()
        y = lax.dot_general(mixed[m], table[m], NT, preferred_element_type=jnp.float32)
        of_row = lax.broadcasted_iota(jnp.int32, y.shape, 0) % k_pad
        of_lane = lax.broadcasted_iota(jnp.int32, y.shape, 1) // lats
        y = jnp.where(of_row == of_lane, y, 0.0)
        for c in range(2):
            total = jnp.sum(y[c * k_pad : (c + 1) * k_pad], axis=0, keepdims=True)
            rows[c * orders + m : c * orders + m + 1, :] = total
        here = slice(m * block, (m + 1) * block)
        re, im, tail_re, tail_im = slot_weights(
            sizes, cols[here], order, quarter, k_lane, r_lane
        )
        re_ref[here] = re.astype(jnp.bfloat16)
        im_ref[here] = im.astype(jnp.bfloat16)
        tail_re_ref[here] = tail_re
        tail_im_ref[here] = tail_im
        if m + 1 < orders:
            mix(m + 1)
    out_ref[...] = rows[...].astype(jnp.bfloat16)


def local_part(alm, beam, wigner, base_index, interp_weights, live_counts, n_strip, n_mr):
    orders, k_count, lats, ells = wigner.shape
    k_pad = -(-k_count // 8) * 8
    lanes = k_count * lats
    slots = base_index.shape[0]
    m_total = orders * n_strip * n_mr
    width = 2 * m_total
    sizes = (2 * m_total, lats, 2 * k_count - 1, 1.0 / math.sqrt(m_total * k_count))
    base = base_index.reshape(1, slots)
    return pl.pallas_call(
        functools.partial(coef_kernel, sizes),
        out_shape=(
            jax.ShapeDtypeStruct((2 * orders, lanes), jnp.bfloat16),
            jax.ShapeDtypeStruct((slots, width), jnp.bfloat16),
            jax.ShapeDtypeStruct((slots, width), jnp.bfloat16),
            jax.ShapeDtypeStruct((slots, lanes), jnp.float32),
            jax.ShapeDtypeStruct((slots, lanes), jnp.float32),
        ),
        in_specs=[pl.BlockSpec(memory_space=pltpu.HBM)] * 6,
        out_specs=(VMEM,) * 5,
        scratch_shapes=[
            pltpu.VMEM(alm.shape, alm.dtype),
            pltpu.VMEM(beam.shape, beam.dtype),
            pltpu.VMEM((orders, lanes, ells), wigner.dtype),
            pltpu.VMEM(interp_weights.shape, interp_weights.dtype),
            pltpu.VMEM(base.shape, base.dtype),
            pltpu.VMEM(live_counts.shape, live_counts.dtype),
            pltpu.VMEM((orders, 2 * k_pad, ells), jnp.bfloat16),
            pltpu.VMEM((2 * orders, lanes), jnp.float32),
            pltpu.VMEM((slots, 16), jnp.float32),
            pltpu.SemaphoreType.DMA((orders + 5,)),
        ],
        compiler_params=pltpu.CompilerParams(vmem_limit_bytes=48 << 20),
        cost_estimate=pl.CostEstimate(
            flops=4 * wigner.size, bytes_accessed=2 * wigner.size, transcendentals=0
        ),
        name="coef",
    )(alm, beam, wigner.reshape(orders, lanes, ells), interp_weights, base, live_counts)


def sample_kernel(re_ref, im_ref, tail_re_ref, tail_im_ref, *refs):
    parts, out_ref, coef = refs[:-2], refs[-2], refs[-1]
    start = 0
    for part in parts:
        coef[start : start + part.shape[0], :] = part[...]
        start += part.shape[0]
    real = jnp.dot(re_ref[...], coef[...], preferred_element_type=jnp.float32)
    imag = jnp.dot(im_ref[...], coef[...], preferred_element_type=jnp.float32)
    terms = real * tail_re_ref[...] + imag * tail_im_ref[...]
    lanes = terms.shape[1]
    whole = lanes // 128 * 128
    total = jnp.zeros((1, terms.shape[0]), jnp.float32)
    if whole:
        tiles = [terms[:, i : i + 128] for i in range(0, whole, 128)]
        total = total + jnp.sum(sum(tiles).T, axis=0, keepdims=True)
    if whole < lanes:
        total = total + jnp.sum(terms[:, whole:].T, axis=0, keepdims=True)
    out_ref[...] = total


def sample(phases, parts):
    slots, width = phases[0].shape
    lanes = phases[2].shape[1]
    block = min(slots, 256)
    rows = lambda n: pl.BlockSpec((block, n), lambda i: (i, 0))
    return pl.pallas_call(
        sample_kernel,
        grid=(slots // block,),
        out_shape=jax.ShapeDtypeStruct((1, slots), jnp.float32),
        in_specs=[rows(width), rows(width), rows(lanes), rows(lanes)]
        + [pl.BlockSpec(part.shape, lambda i: (0, 0)) for part in parts],
        out_specs=pl.BlockSpec((1, block), lambda i: (0, i)),
        scratch_shapes=[pltpu.VMEM((width, lanes), jnp.bfloat16)],
        compiler_params=pltpu.CompilerParams(vmem_limit_bytes=32 << 20),
        cost_estimate=pl.CostEstimate(
            flops=4 * slots * width * lanes, bytes_accessed=1 << 20, transcendentals=0
        ),
        name="sample",
    )(*phases, *parts)


def on_device(alm, beam, wigner, base_index, interp_weights, live_counts):
    n_strip = lax.axis_size("strip")
    n_mr = lax.axis_size("mr")
    mine, *phases = local_part(
        alm, beam, wigner, base_index, interp_weights, live_counts, n_strip, n_mr
    )

    def swap(x, axis, d):
        return lax.ppermute(x, axis, [(i, i ^ d) for i in range(lax.axis_size(axis))])

    column = [swap(mine, "strip", d) for d in range(n_strip - 1, 0, -1)][::-1]
    column = jnp.concatenate([mine] + column, axis=0)
    plane = [column] + [swap(column, "mr", d) for d in range(n_mr - 2, 0, -2)][::-1]
    other = [swap(column, "mr", 1), swap(jnp.concatenate(plane[1:], axis=0), "mr", 1)]
    return sample(phases, plane + other).reshape(-1)


def solution(mesh):
    placed = (
        P(None, ("strip", "mr"), None),
        P(),
        P(("strip", "mr"), None, None, None),
        P(("strip", "mr")),
        P(None, ("strip", "mr")),
        P(("strip", "mr"), None),
    )
    return jax.shard_map(
        on_device, mesh=mesh, in_specs=placed, out_specs=P(("strip", "mr")), check_vma=False
    )
```

```python
import functools
import math

import jax
import jax.numpy as jnp
from jax import lax
from jax.experimental import pallas as pl
from jax.experimental.pallas import tpu as pltpu
from jax.sharding import PartitionSpec as P

NT = (((1,), (1,)), ((), ()))
VMEM = pl.BlockSpec(memory_space=pltpu.VMEM)


def cos_sin_turns(x):
    x = x - jnp.round(x)
    u = x * x
    cos = jnp.zeros_like(x)
    sin = jnp.zeros_like(x)
    for n in range(9, -1, -1):
        cos = cos * u + (-1) ** n * (2 * math.pi) ** (2 * n) / math.factorial(2 * n)
        sin = sin * u + (-1) ** n * (2 * math.pi) ** (2 * n + 1) / math.factorial(2 * n + 1)
    return cos, sin * x


def tap_phases(taps, turns):
    total_re = taps[0] * jnp.ones_like(turns)
    total_im = jnp.zeros_like(total_re)
    for tap in range(1, 4):
        cos, sin = cos_sin_turns(tap * turns)
        total_re = total_re + taps[tap] * cos
        total_im = total_im + taps[tap] * sin
    return total_re, total_im


def turned(turns, values):
    cos, sin = cos_sin_turns(turns)
    return cos * values[0] - sin * values[1], sin * values[0] + cos * values[1]


def divide(x, n):
    quotient = jnp.floor((x + 0.5) * (1.0 / n))
    return quotient, x - n * quotient


def slot_rows(sizes, weights, base, counts, n_strip, n_mr):
    phi_total, lats, psi_count, scale = sizes
    slots = weights.shape[1]
    devices = n_strip * n_mr
    lat_dev, phi_dev = lats // n_mr, phi_total // n_strip
    slot = lax.broadcasted_iota(jnp.int32, (1, slots), 1).astype(jnp.float32)
    dest, at = divide(slot, slots // devices)
    dest_strip, dest_mr = divide(dest, n_mr)
    dests = lax.broadcasted_iota(jnp.int32, (devices, slots), 0).astype(jnp.float32)
    counts = jnp.broadcast_to(counts.astype(jnp.float32), (8, devices)).astype(jnp.bfloat16)
    used = jnp.dot(
        counts, (dests == dest).astype(jnp.bfloat16), preferred_element_type=jnp.float32
    )
    live = (at < used[0:1]).astype(jnp.float32)
    rest, phi_base = divide(base.astype(jnp.float32), phi_dev + 1)
    psi_base, lat_base = divide(rest, lat_dev + 1)
    return jnp.concatenate(
        [
            weights[0:4] * (live * scale),
            weights[4:],
            dest_strip * phi_dev + phi_base - 2.0,
            dest_mr * lat_dev + lat_base - 2.0,
            psi_base,
            jnp.zeros_like(base, jnp.float32),
        ],
        axis=0,
    )


def slot_weights(sizes, cols, order, quarter, k_lane, r_lane):
    phi_total, lats, psi_count, _ = sizes
    col = lambda i: cols[:, i : i + 1]
    turns = order * (1.0 / phi_total)
    phases = turned(col(12) * turns + quarter, tap_phases([col(4 + b) for b in range(4)], turns))
    across = jnp.zeros((cols.shape[0], k_lane.shape[1]), jnp.float32)
    for a in range(4):
        _, row = divide(col(13) + a, lats)
        across = across + jnp.where(row == r_lane, col(a), 0.0)
    tail_re, tail_im = turned(
        divide(col(14) * k_lane, psi_count)[1] * (1.0 / psi_count),
        tap_phases([col(8 + c) for c in range(4)], k_lane * (1.0 / psi_count)),
    )
    return phases + (tail_re * across, -tail_im * across)


def coef_kernel(
    sizes,
    alm_hbm,
    beam_hbm,
    table_hbm,
    weights_hbm,
    base_hbm,
    counts_hbm,
    out_ref,
    re_ref,
    im_ref,
    tail_re_ref,
    tail_im_ref,
    alm,
    beam,
    table,
    weights,
    base,
    counts,
    mixed,
    rows,
    cols,
    sems,
):
    n_strip, n_mr = lax.axis_size("strip"), lax.axis_size("mr")
    orders, lanes, ells = table.shape
    k_count = beam.shape[0]
    lats = lanes // k_count
    k_pad = mixed.shape[1] // 2
    small = [(alm_hbm, alm), (beam_hbm, beam)]
    slot = [(weights_hbm, weights), (base_hbm, base), (counts_hbm, counts)]
    pairs = small + slot + [(table_hbm.at[m], table.at[m]) for m in range(orders)]
    copies = [
        pltpu.make_async_copy(source, target, sems.at[i])
        for i, (source, target) in enumerate(pairs)
    ]
    small, slot, big = copies[:2], copies[2:5], copies[5:]
    for copy in copies:
        copy.start()
    mixed[...] = jnp.zeros_like(mixed)

    width = re_ref.shape[1]
    at = lax.broadcasted_iota(jnp.int32, (1, width), 1).astype(jnp.float32)
    at, m_row = divide(at, orders)
    at, part = divide(at, 2)
    at, strip = divide(at, n_strip)
    core, chip = divide(at, n_mr // 2)
    strip = strip.astype(jnp.int32) ^ lax.axis_index("strip")
    mr = (2.0 * chip + core).astype(jnp.int32) ^ lax.axis_index("mr")
    order = ((strip * n_mr + mr) * orders).astype(jnp.float32) + m_row
    quarter = 0.25 * part
    lane = lax.broadcasted_iota(jnp.int32, (1, lanes), 1).astype(jnp.float32)
    k_lane, r_lane = divide(lane, lats)

    for copy in slot:
        copy.wait()
    cols[...] = slot_rows(sizes, weights[...], base[...], counts[...], n_strip, n_mr).T
    block = cols.shape[0] // orders

    def mix(m):
        for c in range(2):
            product = alm[c, m, :].astype(jnp.float32)[None, :] * beam[...]
            mixed[m, c * k_pad : c * k_pad + k_count, :] = product.astype(jnp.bfloat16)

    for copy in small:
        copy.wait()
    mix(0)
    for m in range(orders):
        big[m].wait()
        y = lax.dot_general(mixed[m], table[m], NT, preferred_element_type=jnp.float32)
        of_row = lax.broadcasted_iota(jnp.int32, y.shape, 0) % k_pad
        of_lane = lax.broadcasted_iota(jnp.int32, y.shape, 1) // lats
        y = jnp.where(of_row == of_lane, y, 0.0)
        for c in range(2):
            total = jnp.sum(y[c * k_pad : (c + 1) * k_pad], axis=0, keepdims=True)
            rows[c * orders + m : c * orders + m + 1, :] = total
        here = slice(m * block, (m + 1) * block)
        re, im, tail_re, tail_im = slot_weights(
            sizes, cols[here], order, quarter, k_lane, r_lane
        )
        re_ref[here] = re.astype(jnp.bfloat16)
        im_ref[here] = im.astype(jnp.bfloat16)
        tail_re_ref[here] = tail_re
        tail_im_ref[here] = tail_im
        if m + 1 < orders:
            mix(m + 1)
    out_ref[...] = rows[...].astype(jnp.bfloat16)


def local_part(alm, beam, wigner, base_index, interp_weights, live_counts, n_strip, n_mr):
    orders, k_count, lats, ells = wigner.shape
    k_pad = -(-k_count // 8) * 8
    lanes = k_count * lats
    slots = base_index.shape[0]
    m_total = orders * n_strip * n_mr
    width = 2 * m_total
    sizes = (2 * m_total, lats, 2 * k_count - 1, 1.0 / math.sqrt(m_total * k_count))
    base = base_index.reshape(1, slots)
    return pl.pallas_call(
        functools.partial(coef_kernel, sizes),
        out_shape=(
            jax.ShapeDtypeStruct((2 * orders, lanes), jnp.bfloat16),
            jax.ShapeDtypeStruct((slots, width), jnp.bfloat16),
            jax.ShapeDtypeStruct((slots, width), jnp.bfloat16),
            jax.ShapeDtypeStruct((slots, lanes), jnp.float32),
            jax.ShapeDtypeStruct((slots, lanes), jnp.float32),
        ),
        in_specs=[pl.BlockSpec(memory_space=pltpu.HBM)] * 6,
        out_specs=(VMEM,) * 5,
        scratch_shapes=[
            pltpu.VMEM(alm.shape, alm.dtype),
            pltpu.VMEM(beam.shape, beam.dtype),
            pltpu.VMEM((orders, lanes, ells), wigner.dtype),
            pltpu.VMEM(interp_weights.shape, interp_weights.dtype),
            pltpu.VMEM(base.shape, base.dtype),
            pltpu.VMEM(live_counts.shape, live_counts.dtype),
            pltpu.VMEM((orders, 2 * k_pad, ells), jnp.bfloat16),
            pltpu.VMEM((2 * orders, lanes), jnp.float32),
            pltpu.VMEM((slots, 16), jnp.float32),
            pltpu.SemaphoreType.DMA((orders + 5,)),
        ],
        compiler_params=pltpu.CompilerParams(vmem_limit_bytes=48 << 20),
        cost_estimate=pl.CostEstimate(
            flops=4 * wigner.size, bytes_accessed=2 * wigner.size, transcendentals=0
        ),
        name="coef",
    )(
        *(
            pltpu.with_memory_space_constraint(x, pltpu.HBM)
            for x in (
                alm,
                beam,
                wigner.reshape(orders, lanes, ells),
                interp_weights,
                base,
                live_counts,
            )
        )
    )


def sample_kernel(re_ref, im_ref, tail_re_ref, tail_im_ref, *refs):
    parts, out_ref, coef = refs[:-2], refs[-2], refs[-1]
    start = 0
    for part in parts:
        coef[start : start + part.shape[0], :] = part[...]
        start += part.shape[0]
    real = jnp.dot(re_ref[...], coef[...], preferred_element_type=jnp.float32)
    imag = jnp.dot(im_ref[...], coef[...], preferred_element_type=jnp.float32)
    terms = real * tail_re_ref[...] + imag * tail_im_ref[...]
    lanes = terms.shape[1]
    whole = lanes // 128 * 128
    total = jnp.zeros((1, terms.shape[0]), jnp.float32)
    if whole:
        tiles = [terms[:, i : i + 128] for i in range(0, whole, 128)]
        total = total + jnp.sum(sum(tiles).T, axis=0, keepdims=True)
    if whole < lanes:
        total = total + jnp.sum(terms[:, whole:].T, axis=0, keepdims=True)
    out_ref[...] = total


def sample(phases, parts):
    slots, width = phases[0].shape
    lanes = phases[2].shape[1]
    block = min(slots, 256)
    rows = lambda n: pl.BlockSpec((block, n), lambda i: (i, 0))
    return pl.pallas_call(
        sample_kernel,
        grid=(slots // block,),
        out_shape=jax.ShapeDtypeStruct((1, slots), jnp.float32),
        in_specs=[rows(width), rows(width), rows(lanes), rows(lanes)]
        + [pl.BlockSpec(part.shape, lambda i: (0, 0)) for part in parts],
        out_specs=pl.BlockSpec((1, block), lambda i: (0, i)),
        scratch_shapes=[pltpu.VMEM((width, lanes), jnp.bfloat16)],
        compiler_params=pltpu.CompilerParams(vmem_limit_bytes=32 << 20),
        cost_estimate=pl.CostEstimate(
            flops=4 * slots * width * lanes, bytes_accessed=1 << 20, transcendentals=0
        ),
        name="sample",
    )(*phases, *parts)


def on_device(alm, beam, wigner, base_index, interp_weights, live_counts):
    n_strip = lax.axis_size("strip")
    n_mr = lax.axis_size("mr")
    mine, *phases = local_part(
        alm, beam, wigner, base_index, interp_weights, live_counts, n_strip, n_mr
    )

    def swap(x, axis, d):
        return lax.ppermute(x, axis, [(i, i ^ d) for i in range(lax.axis_size(axis))])

    column = [swap(mine, "strip", d) for d in range(n_strip - 1, 0, -1)][::-1]
    column = jnp.concatenate([mine] + column, axis=0)
    plane = [column] + [swap(column, "mr", d) for d in range(n_mr - 2, 0, -2)][::-1]
    other = [swap(part, "mr", 1) for part in plane]
    return sample(phases, plane + other).reshape(-1)


def solution(mesh):
    placed = (
        P(None, ("strip", "mr"), None),
        P(),
        P(("strip", "mr"), None, None, None),
        P(("strip", "mr")),
        P(None, ("strip", "mr")),
        P(("strip", "mr"), None),
    )
    return jax.shard_map(
        on_device, mesh=mesh, in_specs=placed, out_specs=P(("strip", "mr")), check_vma=False
    )
```

```python
import functools
import math

import jax
import jax.numpy as jnp
from jax import lax
from jax.experimental import pallas as pl
from jax.experimental.pallas import tpu as pltpu
from jax.sharding import PartitionSpec as P

NT = (((1,), (1,)), ((), ()))
LANES = 128
VMEM = pl.BlockSpec(memory_space=pltpu.VMEM)


def cos_sin_turns(x):
    x = x - jnp.round(x)
    u = x * x
    cos = jnp.zeros_like(x)
    sin = jnp.zeros_like(x)
    for n in range(9, -1, -1):
        cos = cos * u + (-1) ** n * (2 * math.pi) ** (2 * n) / math.factorial(2 * n)
        sin = sin * u + (-1) ** n * (2 * math.pi) ** (2 * n + 1) / math.factorial(2 * n + 1)
    return cos, sin * x


def times(x, y):
    return x[0] * y[0] - x[1] * y[1], x[1] * y[0] + x[0] * y[1]


def tap_steps(turns):
    return [cos_sin_turns(tap * turns) for tap in range(1, 4)]


def tap_sum(taps, steps):
    re = taps[0] + taps[1] * steps[0][0] + taps[2] * steps[1][0] + taps[3] * steps[2][0]
    im = taps[1] * steps[0][1] + taps[2] * steps[1][1] + taps[3] * steps[2][1]
    return re, im


def divide(x, n):
    quotient = jnp.floor((x + 0.5) * (1.0 / n))
    return quotient, x - n * quotient


def slot_rows(sizes, weights, base, counts, n_strip, n_mr):
    phi_total, lats, psi_count, scale = sizes
    slots = weights.shape[1]
    devices = n_strip * n_mr
    lat_dev, phi_dev = lats // n_mr, phi_total // n_strip
    slot = lax.broadcasted_iota(jnp.int32, (1, slots), 1).astype(jnp.float32)
    dest, at = divide(slot, slots // devices)
    dest_strip, dest_mr = divide(dest, n_mr)
    dests = lax.broadcasted_iota(jnp.int32, (devices, slots), 0).astype(jnp.float32)
    counts = jnp.broadcast_to(counts.astype(jnp.float32), (8, devices)).astype(jnp.bfloat16)
    used = jnp.dot(
        counts, (dests == dest).astype(jnp.bfloat16), preferred_element_type=jnp.float32
    )
    live = (at < used[0:1]).astype(jnp.float32)
    rest, phi_base = divide(base.astype(jnp.float32), phi_dev + 1)
    psi_base, lat_base = divide(rest, lat_dev + 1)
    return jnp.concatenate(
        [
            weights[0:4] * (live * scale),
            weights[4:],
            dest_strip * phi_dev + phi_base - 2.0,
            dest_mr * lat_dev + lat_base - 2.0,
            psi_base,
            jnp.zeros_like(base, jnp.float32),
        ],
        axis=0,
    )


def lane_row():
    return lax.broadcasted_iota(jnp.int32, (1, LANES), 1).astype(jnp.float32)


def spread(values, first, each):
    index = lax.broadcasted_iota(jnp.int32, values.shape, 1) // each + first
    return jnp.take_along_axis(values, index, axis=1)


def fixed_rows(sizes, n_strip, n_mr, orders, width):
    phi_total, _, psi_count, _ = sizes

    def first_order(source):
        at, strip = divide(source, n_strip)
        core, chip = divide(at, n_mr // 2)
        strip = strip.astype(jnp.int32) ^ lax.axis_index("strip")
        mr = (2.0 * chip + core).astype(jnp.int32) ^ lax.axis_index("mr")
        return ((strip * n_mr + mr) * orders).astype(jnp.float32)

    column = lax.broadcasted_iota(jnp.int32, (1, width), 1).astype(jnp.float32)
    at, m_there = divide(column, orders)
    source, _ = divide(at, 2)
    order = first_order(source) + m_there
    _, source = divide(lane_row(), n_strip * n_mr)
    at, m_here = divide(lane_row(), orders)
    _, part = divide(at, 2)
    return (
        first_order(source) * (1.0 / phi_total),
        m_here * (1.0 / phi_total),
        0.25 * part,
        tap_steps(order * (1.0 / phi_total)),
        tap_steps(lane_row() * (1.0 / psi_count)),
    )


def slot_weights(sizes, cols, fixed, orders, refs, here):
    _, lats, psi_count, _ = sizes
    source_turns, own_turns, quarter, phi_steps, psi_steps = fixed
    re_ref, im_ref, tail_re_ref, tail_im_ref = refs
    col = [jnp.broadcast_to(cols[:, i : i + 1], (cols.shape[0], LANES)) for i in range(15)]
    source = cos_sin_turns(col[12] * source_turns)
    own = cos_sin_turns(col[12] * own_turns + quarter)
    for tile in range(0, re_ref.shape[1], LANES):
        there = slice(tile, tile + LANES)
        first = tile // (2 * orders)
        steps = [(cos[:, there], sin[:, there]) for cos, sin in phi_steps]
        turn = times(own, [spread(x, first, 2 * orders) for x in source])
        re, im = times(turn, tap_sum(col[4:8], steps))
        re_ref[here, there] = re.astype(jnp.bfloat16)
        im_ref[here, there] = im.astype(jnp.bfloat16)
    _, r_lane = divide(lane_row(), lats)
    across = jnp.zeros_like(col[0])
    for a in range(4):
        _, row = divide(col[13] + a, lats)
        across = across + jnp.where(row == r_lane, col[a], 0.0)
    _, psi_turns = divide(col[14] * lane_row(), psi_count)
    turn = cos_sin_turns(psi_turns * (1.0 / psi_count))
    along_re, along_im = times(turn, tap_sum(col[8:12], psi_steps))
    for tile in range(0, tail_re_ref.shape[1], LANES):
        there = slice(tile, min(tile + LANES, tail_re_ref.shape[1]))
        size = there.stop - there.start
        first = tile // lats
        tail_re_ref[here, there] = (spread(along_re, first, lats) * across)[:, :size]
        tail_im_ref[here, there] = -(spread(along_im, first, lats) * across)[:, :size]


def coef_kernel(
    sizes,
    alm_hbm,
    beam_hbm,
    table_hbm,
    weights_hbm,
    base_hbm,
    counts_hbm,
    out_ref,
    re_ref,
    im_ref,
    tail_re_ref,
    tail_im_ref,
    alm,
    beam,
    table,
    weights,
    base,
    counts,
    mixed,
    rows,
    cols,
    sems,
):
    n_strip, n_mr = lax.axis_size("strip"), lax.axis_size("mr")
    orders, lanes, ells = table.shape
    k_count = beam.shape[0]
    lats = lanes // k_count
    k_pad = mixed.shape[1] // 2
    small = [(alm_hbm, alm), (beam_hbm, beam)]
    slot = [(weights_hbm, weights), (base_hbm, base), (counts_hbm, counts)]
    pairs = small + slot + [(table_hbm.at[m], table.at[m]) for m in range(orders)]
    copies = [
        pltpu.make_async_copy(source, target, sems.at[i])
        for i, (source, target) in enumerate(pairs)
    ]
    small, slot, big = copies[:2], copies[2:5], copies[5:]
    for copy in copies:
        copy.start()
    mixed[...] = jnp.zeros_like(mixed)

    fixed = fixed_rows(sizes, n_strip, n_mr, orders, re_ref.shape[1])
    for copy in slot:
        copy.wait()
    cols[...] = slot_rows(sizes, weights[...], base[...], counts[...], n_strip, n_mr).T
    block = cols.shape[0] // orders

    def mix(m):
        for c in range(2):
            product = alm[c, m, :].astype(jnp.float32)[None, :] * beam[...]
            mixed[m, c * k_pad : c * k_pad + k_count, :] = product.astype(jnp.bfloat16)

    for copy in small:
        copy.wait()
    mix(0)
    steps = [[0]] + [[m, m + 1] for m in range(1, orders - 1, 2)] + [[orders - 1]]
    for step in steps:
        for m in step:
            big[m].wait()
        for m in step:
            y = lax.dot_general(mixed[m], table[m], NT, preferred_element_type=jnp.float32)
            of_row = lax.broadcasted_iota(jnp.int32, y.shape, 0) % k_pad
            of_lane = lax.broadcasted_iota(jnp.int32, y.shape, 1) // lats
            y = jnp.where(of_row == of_lane, y, 0.0)
            for c in range(2):
                total = jnp.sum(y[c * k_pad : (c + 1) * k_pad], axis=0, keepdims=True)
                rows[c * orders + m : c * orders + m + 1, :] = total
        for m in step:
            here = slice(m * block, (m + 1) * block)
            slot_weights(
                sizes,
                cols[here],
                fixed,
                orders,
                (re_ref, im_ref, tail_re_ref, tail_im_ref),
                here,
            )
        for m in range(step[-1] + 1, min(step[-1] + 3, orders)):
            mix(m)
    out_ref[...] = rows[...].astype(jnp.bfloat16)


def local_part(alm, beam, wigner, base_index, interp_weights, live_counts, n_strip, n_mr):
    orders, k_count, lats, ells = wigner.shape
    k_pad = -(-k_count // 8) * 8
    lanes = k_count * lats
    slots = base_index.shape[0]
    m_total = orders * n_strip * n_mr
    width = 2 * m_total
    sizes = (2 * m_total, lats, 2 * k_count - 1, 1.0 / math.sqrt(m_total * k_count))
    base = base_index.reshape(1, slots)
    return pl.pallas_call(
        functools.partial(coef_kernel, sizes),
        out_shape=(
            jax.ShapeDtypeStruct((2 * orders, lanes), jnp.bfloat16),
            jax.ShapeDtypeStruct((slots, width), jnp.bfloat16),
            jax.ShapeDtypeStruct((slots, width), jnp.bfloat16),
            jax.ShapeDtypeStruct((slots, lanes), jnp.float32),
            jax.ShapeDtypeStruct((slots, lanes), jnp.float32),
        ),
        in_specs=[pl.BlockSpec(memory_space=pltpu.HBM)] * 6,
        out_specs=(VMEM,) * 5,
        scratch_shapes=[
            pltpu.VMEM(alm.shape, alm.dtype),
            pltpu.VMEM(beam.shape, beam.dtype),
            pltpu.VMEM((orders, lanes, ells), wigner.dtype),
            pltpu.VMEM(interp_weights.shape, interp_weights.dtype),
            pltpu.VMEM(base.shape, base.dtype),
            pltpu.VMEM(live_counts.shape, live_counts.dtype),
            pltpu.VMEM((orders, 2 * k_pad, ells), jnp.bfloat16),
            pltpu.VMEM((2 * orders, lanes), jnp.float32),
            pltpu.VMEM((slots, 16), jnp.float32),
            pltpu.SemaphoreType.DMA((orders + 5,)),
        ],
        compiler_params=pltpu.CompilerParams(vmem_limit_bytes=48 << 20),
        cost_estimate=pl.CostEstimate(
            flops=4 * wigner.size, bytes_accessed=2 * wigner.size, transcendentals=0
        ),
        name="coef",
    )(
        *(
            pltpu.with_memory_space_constraint(x, pltpu.HBM)
            for x in (
                alm,
                beam,
                wigner.reshape(orders, lanes, ells),
                interp_weights,
                base,
                live_counts,
            )
        )
    )


def sample_kernel(re_ref, im_ref, tail_re_ref, tail_im_ref, *refs):
    parts, out_ref, coef = refs[:-2], refs[-2], refs[-1]
    start = 0
    for part in parts:
        coef[start : start + part.shape[0], :] = part[...]
        start += part.shape[0]
    both = jnp.concatenate([re_ref[...], im_ref[...]], axis=0)
    both = jnp.dot(both, coef[...], preferred_element_type=jnp.float32)
    slots = re_ref.shape[0]
    terms = both[:slots] * tail_re_ref[...] + both[slots:] * tail_im_ref[...]
    lanes = terms.shape[1]
    whole = lanes // 128 * 128
    total = jnp.zeros((1, terms.shape[0]), jnp.float32)
    if whole:
        tiles = [terms[:, i : i + 128] for i in range(0, whole, 128)]
        total = total + jnp.sum(sum(tiles).T, axis=0, keepdims=True)
    if whole < lanes:
        total = total + jnp.sum(terms[:, whole:].T, axis=0, keepdims=True)
    out_ref[...] = total


def sample(phases, parts):
    slots, width = phases[0].shape
    lanes = phases[2].shape[1]
    block = min(slots, 256)
    rows = lambda n: pl.BlockSpec((block, n), lambda i: (i, 0))
    return pl.pallas_call(
        sample_kernel,
        grid=(slots // block,),
        out_shape=jax.ShapeDtypeStruct((1, slots), jnp.float32),
        in_specs=[rows(width), rows(width), rows(lanes), rows(lanes)]
        + [pl.BlockSpec(part.shape, lambda i: (0, 0)) for part in parts],
        out_specs=pl.BlockSpec((1, block), lambda i: (0, i)),
        scratch_shapes=[pltpu.VMEM((width, lanes), jnp.bfloat16)],
        compiler_params=pltpu.CompilerParams(vmem_limit_bytes=32 << 20),
        cost_estimate=pl.CostEstimate(
            flops=4 * slots * width * lanes, bytes_accessed=1 << 20, transcendentals=0
        ),
        name="sample",
    )(*phases, *parts)


def on_device(alm, beam, wigner, base_index, interp_weights, live_counts):
    n_strip = lax.axis_size("strip")
    n_mr = lax.axis_size("mr")
    mine, *phases = local_part(
        alm, beam, wigner, base_index, interp_weights, live_counts, n_strip, n_mr
    )

    def swap(x, axis, d):
        return lax.ppermute(x, axis, [(i, i ^ d) for i in range(lax.axis_size(axis))])

    column = [swap(mine, "strip", d) for d in range(n_strip - 1, 0, -1)][::-1]
    column = jnp.concatenate([mine] + column, axis=0)
    plane = [column] + [swap(column, "mr", d) for d in range(n_mr - 2, 0, -2)][::-1]
    other = [swap(part, "mr", 1) for part in plane]
    return sample(phases, plane + other).reshape(-1)


def solution(mesh):
    placed = (
        P(None, ("strip", "mr"), None),
        P(),
        P(("strip", "mr"), None, None, None),
        P(("strip", "mr")),
        P(None, ("strip", "mr")),
        P(("strip", "mr"), None),
    )
    return jax.shard_map(
        on_device, mesh=mesh, in_specs=placed, out_specs=P(("strip", "mr")), check_vma=False
    )
```

```python
import functools
import math

import jax
import jax.numpy as jnp
from jax import lax
from jax.experimental import pallas as pl
from jax.experimental.pallas import tpu as pltpu
from jax.sharding import PartitionSpec as P

NT = (((1,), (1,)), ((), ()))
LANES = 128
VMEM = pl.BlockSpec(memory_space=pltpu.VMEM)


def cos_sin_turns(x):
    x = x - jnp.round(x)
    u = x * x
    cos = jnp.zeros_like(x)
    sin = jnp.zeros_like(x)
    for n in range(9, -1, -1):
        cos = cos * u + (-1) ** n * (2 * math.pi) ** (2 * n) / math.factorial(2 * n)
        sin = sin * u + (-1) ** n * (2 * math.pi) ** (2 * n + 1) / math.factorial(2 * n + 1)
    return cos, sin * x


def times(x, y):
    return x[0] * y[0] - x[1] * y[1], x[1] * y[0] + x[0] * y[1]


def tap_steps(turns):
    return [cos_sin_turns(tap * turns) for tap in range(1, 4)]


def tap_sum(taps, steps):
    re = taps[0] + taps[1] * steps[0][0] + taps[2] * steps[1][0] + taps[3] * steps[2][0]
    im = taps[1] * steps[0][1] + taps[2] * steps[1][1] + taps[3] * steps[2][1]
    return re, im


def divide(x, n):
    quotient = jnp.floor((x + 0.5) * (1.0 / n))
    return quotient, x - n * quotient


def slot_rows(sizes, weights, base, counts, n_strip, n_mr):
    phi_total, lats, psi_count, scale = sizes
    slots = weights.shape[1]
    devices = n_strip * n_mr
    lat_dev, phi_dev = lats // n_mr, phi_total // n_strip
    slot = lax.broadcasted_iota(jnp.int32, (1, slots), 1).astype(jnp.float32)
    dest, at = divide(slot, slots // devices)
    dest_strip, dest_mr = divide(dest, n_mr)
    dests = lax.broadcasted_iota(jnp.int32, (devices, slots), 0).astype(jnp.float32)
    counts = jnp.broadcast_to(counts.astype(jnp.float32), (8, devices)).astype(jnp.bfloat16)
    used = jnp.dot(
        counts, (dests == dest).astype(jnp.bfloat16), preferred_element_type=jnp.float32
    )
    live = (at < used[0:1]).astype(jnp.float32)
    rest, phi_base = divide(base.astype(jnp.float32), phi_dev + 1)
    psi_base, lat_base = divide(rest, lat_dev + 1)
    return jnp.concatenate(
        [
            weights[0:4] * (live * scale),
            weights[4:],
            dest_strip * phi_dev + phi_base - 2.0,
            dest_mr * lat_dev + lat_base - 2.0,
            psi_base,
            jnp.zeros_like(base, jnp.float32),
        ],
        axis=0,
    )


def lane_row():
    return lax.broadcasted_iota(jnp.int32, (1, LANES), 1).astype(jnp.float32)


def spread(values, first, each):
    index = lax.broadcasted_iota(jnp.int32, values.shape, 1) // each + first
    return jnp.take_along_axis(values, index, axis=1)


def fixed_rows(sizes, n_strip, n_mr, orders, width):
    phi_total, _, psi_count, _ = sizes

    def first_order(source):
        at, strip = divide(source, n_strip)
        core, chip = divide(at, n_mr // 2)
        strip = strip.astype(jnp.int32) ^ lax.axis_index("strip")
        _, chip = divide(n_mr // 2 - chip, n_mr // 2)
        mr = (2.0 * chip + core).astype(jnp.int32) ^ lax.axis_index("mr")
        return ((strip * n_mr + mr) * orders).astype(jnp.float32)

    column = lax.broadcasted_iota(jnp.int32, (1, width), 1).astype(jnp.float32)
    at, m_there = divide(column, orders)
    source, _ = divide(at, 2)
    order = first_order(source) + m_there
    _, source = divide(lane_row(), n_strip * n_mr)
    at, m_here = divide(lane_row(), orders)
    _, part = divide(at, 2)
    return (
        first_order(source) * (1.0 / phi_total),
        m_here * (1.0 / phi_total),
        0.25 * part,
        tap_steps(order * (1.0 / phi_total)),
        tap_steps(lane_row() * (1.0 / psi_count)),
    )


def slot_weights(sizes, cols, fixed, orders, refs, here):
    _, lats, psi_count, _ = sizes
    source_turns, own_turns, quarter, phi_steps, psi_steps = fixed
    re_ref, im_ref, tail_re_ref, tail_im_ref = refs
    col = [jnp.broadcast_to(cols[:, i : i + 1], (cols.shape[0], LANES)) for i in range(15)]
    source = cos_sin_turns(col[12] * source_turns)
    own = cos_sin_turns(col[12] * own_turns + quarter)
    for tile in range(0, re_ref.shape[1], LANES):
        there = slice(tile, tile + LANES)
        first = tile // (2 * orders)
        steps = [(cos[:, there], sin[:, there]) for cos, sin in phi_steps]
        turn = times(own, [spread(x, first, 2 * orders) for x in source])
        re, im = times(turn, tap_sum(col[4:8], steps))
        re_ref[here, there] = re.astype(jnp.bfloat16)
        im_ref[here, there] = im.astype(jnp.bfloat16)
    _, r_lane = divide(lane_row(), lats)
    across = jnp.zeros_like(col[0])
    for a in range(4):
        _, row = divide(col[13] + a, lats)
        across = across + jnp.where(row == r_lane, col[a], 0.0)
    _, psi_turns = divide(col[14] * lane_row(), psi_count)
    turn = cos_sin_turns(psi_turns * (1.0 / psi_count))
    along_re, along_im = times(turn, tap_sum(col[8:12], psi_steps))
    for tile in range(0, tail_re_ref.shape[1], LANES):
        there = slice(tile, min(tile + LANES, tail_re_ref.shape[1]))
        size = there.stop - there.start
        first = tile // lats
        tail_re_ref[here, there] = (spread(along_re, first, lats) * across)[:, :size]
        tail_im_ref[here, there] = -(spread(along_im, first, lats) * across)[:, :size]


def coef_kernel(
    sizes,
    alm_hbm,
    beam_hbm,
    table_hbm,
    weights_hbm,
    base_hbm,
    counts_hbm,
    out_ref,
    re_ref,
    im_ref,
    tail_re_ref,
    tail_im_ref,
    alm,
    beam,
    table,
    weights,
    base,
    counts,
    mixed,
    rows,
    cols,
    sems,
):
    n_strip, n_mr = lax.axis_size("strip"), lax.axis_size("mr")
    orders, lanes, ells = table.shape
    k_count = beam.shape[0]
    lats = lanes // k_count
    k_pad = mixed.shape[1] // 2
    small = [(alm_hbm, alm), (beam_hbm, beam)]
    slot = [(weights_hbm, weights), (base_hbm, base), (counts_hbm, counts)]
    pairs = small + slot + [(table_hbm.at[m], table.at[m]) for m in range(orders)]
    copies = [
        pltpu.make_async_copy(source, target, sems.at[i])
        for i, (source, target) in enumerate(pairs)
    ]
    small, slot, big = copies[:2], copies[2:5], copies[5:]
    for copy in copies:
        copy.start()
    mixed[...] = jnp.zeros_like(mixed)

    fixed = fixed_rows(sizes, n_strip, n_mr, orders, re_ref.shape[1])
    for copy in slot:
        copy.wait()
    cols[...] = slot_rows(sizes, weights[...], base[...], counts[...], n_strip, n_mr).T
    block = cols.shape[0] // orders

    def mix(m):
        for c in range(2):
            product = alm[c, m, :].astype(jnp.float32)[None, :] * beam[...]
            mixed[m, c * k_pad : c * k_pad + k_count, :] = product.astype(jnp.bfloat16)

    for copy in small:
        copy.wait()
    mix(0)
    steps = [[0]] + [[m, m + 1] for m in range(1, orders - 1, 2)] + [[orders - 1]]
    for at, step in enumerate(steps):
        for m in step:
            big[m].wait()
        for m in step:
            y = lax.dot_general(mixed[m], table[m], NT, preferred_element_type=jnp.float32)
            of_row = lax.broadcasted_iota(jnp.int32, y.shape, 0) % k_pad
            of_lane = lax.broadcasted_iota(jnp.int32, y.shape, 1) // lats
            y = jnp.where(of_row == of_lane, y, 0.0)
            for c in range(2):
                total = jnp.sum(y[c * k_pad : (c + 1) * k_pad], axis=0, keepdims=True)
                rows[c * orders + m : c * orders + m + 1, :] = total
        for m in range(2 * at, min(2 * at + 2, orders)):
            here = slice(m * block, (m + 1) * block)
            slot_weights(
                sizes,
                cols[here],
                fixed,
                orders,
                (re_ref, im_ref, tail_re_ref, tail_im_ref),
                here,
            )
        for m in range(step[-1] + 1, min(step[-1] + 3, orders)):
            mix(m)
    out_ref[...] = rows[...].astype(jnp.bfloat16)


def local_part(alm, beam, wigner, base_index, interp_weights, live_counts, n_strip, n_mr):
    orders, k_count, lats, ells = wigner.shape
    k_pad = -(-k_count // 8) * 8
    lanes = k_count * lats
    slots = base_index.shape[0]
    m_total = orders * n_strip * n_mr
    width = 2 * m_total
    sizes = (2 * m_total, lats, 2 * k_count - 1, 1.0 / math.sqrt(m_total * k_count))
    base = base_index.reshape(1, slots)
    return pl.pallas_call(
        functools.partial(coef_kernel, sizes),
        out_shape=(
            jax.ShapeDtypeStruct((2 * orders, lanes), jnp.bfloat16),
            jax.ShapeDtypeStruct((slots, width), jnp.bfloat16),
            jax.ShapeDtypeStruct((slots, width), jnp.bfloat16),
            jax.ShapeDtypeStruct((slots, lanes), jnp.float32),
            jax.ShapeDtypeStruct((slots, lanes), jnp.float32),
        ),
        in_specs=[pl.BlockSpec(memory_space=pltpu.HBM)] * 6,
        out_specs=(VMEM,) * 5,
        scratch_shapes=[
            pltpu.VMEM(alm.shape, alm.dtype),
            pltpu.VMEM(beam.shape, beam.dtype),
            pltpu.VMEM((orders, lanes, ells), wigner.dtype),
            pltpu.VMEM(interp_weights.shape, interp_weights.dtype),
            pltpu.VMEM(base.shape, base.dtype),
            pltpu.VMEM(live_counts.shape, live_counts.dtype),
            pltpu.VMEM((orders, 2 * k_pad, ells), jnp.bfloat16),
            pltpu.VMEM((2 * orders, lanes), jnp.float32),
            pltpu.VMEM((slots, 16), jnp.float32),
            pltpu.SemaphoreType.DMA((orders + 5,)),
        ],
        compiler_params=pltpu.CompilerParams(vmem_limit_bytes=48 << 20),
        cost_estimate=pl.CostEstimate(
            flops=4 * wigner.size, bytes_accessed=2 * wigner.size, transcendentals=0
        ),
        name="coef",
    )(
        *(
            pltpu.with_memory_space_constraint(x, pltpu.HBM)
            for x in (
                alm,
                beam,
                wigner.reshape(orders, lanes, ells),
                interp_weights,
                base,
                live_counts,
            )
        )
    )


def sample_kernel(first, re_ref, im_ref, tail_re_ref, tail_im_ref, *refs):
    *parts, before_ref, out_ref, coef = refs
    start = 0
    for part in parts:
        coef[start : start + part.shape[0], :] = part[...]
        start += part.shape[0]
    slots, lanes = tail_re_ref.shape
    block = min(slots, 256)
    whole = lanes // LANES * LANES
    for i in range(0, slots, block):
        here = slice(i, i + block)
        both = [ref[here, first : first + start] for ref in (re_ref, im_ref)]
        both = jnp.concatenate(both, axis=0)
        both = jnp.dot(both, coef[...], preferred_element_type=jnp.float32)
        terms = both[:block] * tail_re_ref[here] + both[block:] * tail_im_ref[here]
        total = before_ref[:, here]
        if whole:
            tiles = [terms[:, j : j + LANES] for j in range(0, whole, LANES)]
            total = total + jnp.sum(sum(tiles).T, axis=0, keepdims=True)
        if whole < lanes:
            total = total + jnp.sum(terms[:, whole:].T, axis=0, keepdims=True)
        out_ref[:, here] = total


def sample(phases, first, parts, before):
    slots, lanes = phases[2].shape
    rows = sum(part.shape[0] for part in parts)
    return pl.pallas_call(
        functools.partial(sample_kernel, first),
        out_shape=jax.ShapeDtypeStruct((1, slots), jnp.float32),
        in_specs=[VMEM] * (5 + len(parts)),
        out_specs=VMEM,
        scratch_shapes=[pltpu.VMEM((rows, lanes), jnp.bfloat16)],
        compiler_params=pltpu.CompilerParams(vmem_limit_bytes=32 << 20),
        cost_estimate=pl.CostEstimate(
            flops=4 * slots * rows * lanes, bytes_accessed=1 << 20, transcendentals=0
        ),
        name="sample",
    )(*phases, *parts, before)


def on_device(alm, beam, wigner, base_index, interp_weights, live_counts):
    n_strip = lax.axis_size("strip")
    n_mr = lax.axis_size("mr")
    mine, *phases = local_part(
        alm, beam, wigner, base_index, interp_weights, live_counts, n_strip, n_mr
    )

    def swap(x, axis, d):
        return lax.ppermute(x, axis, [(i, i ^ d) for i in range(lax.axis_size(axis))])

    column = [swap(mine, "strip", d) for d in range(n_strip - 1, 0, -1)][::-1]
    column = jnp.concatenate([mine] + column, axis=0)
    plane = [column] + [swap(column, "mr", d) for d in range(n_mr - 2, 0, -2)]
    other = [swap(part, "mr", 1) for part in plane]
    parts = plane + other
    early, late = parts[:-2], parts[-2:]
    zero = jnp.zeros((1, base_index.shape[0]), jnp.float32)
    result = sample(phases, 0, early, zero)
    result = sample(phases, sum(part.shape[0] for part in early), late, result)
    return result.reshape(-1)


def solution(mesh):
    placed = (
        P(None, ("strip", "mr"), None),
        P(),
        P(("strip", "mr"), None, None, None),
        P(("strip", "mr")),
        P(None, ("strip", "mr")),
        P(("strip", "mr"), None),
    )
    return jax.shard_map(
        on_device, mesh=mesh, in_specs=placed, out_specs=P(("strip", "mr")), check_vma=False
    )
```

```python
import functools
import math

import jax
import jax.numpy as jnp
from jax import lax
from jax.experimental import pallas as pl
from jax.experimental.pallas import tpu as pltpu
from jax.sharding import PartitionSpec as P

NT = (((1,), (1,)), ((), ()))
LANES = 128
VMEM = pl.BlockSpec(memory_space=pltpu.VMEM)


def cos_sin_turns(x):
    x = x - jnp.round(x)
    u = x * x
    cos = jnp.zeros_like(x)
    sin = jnp.zeros_like(x)
    for n in range(9, -1, -1):
        cos = cos * u + (-1) ** n * (2 * math.pi) ** (2 * n) / math.factorial(2 * n)
        sin = sin * u + (-1) ** n * (2 * math.pi) ** (2 * n + 1) / math.factorial(2 * n + 1)
    return cos, sin * x


def times(x, y):
    return x[0] * y[0] - x[1] * y[1], x[1] * y[0] + x[0] * y[1]


def tap_steps(turns):
    return [cos_sin_turns(tap * turns) for tap in range(1, 4)]


def tap_sum(taps, steps):
    re = taps[0] + taps[1] * steps[0][0] + taps[2] * steps[1][0] + taps[3] * steps[2][0]
    im = taps[1] * steps[0][1] + taps[2] * steps[1][1] + taps[3] * steps[2][1]
    return re, im


def divide(x, n):
    quotient = jnp.floor((x + 0.5) * (1.0 / n))
    return quotient, x - n * quotient


def slot_rows(sizes, weights, base, counts, n_strip, n_mr):
    phi_total, lats, psi_count, scale = sizes
    slots = weights.shape[1]
    devices = n_strip * n_mr
    lat_dev, phi_dev = lats // n_mr, phi_total // n_strip
    slot = lax.broadcasted_iota(jnp.int32, (1, slots), 1).astype(jnp.float32)
    dest, at = divide(slot, slots // devices)
    dest_strip, dest_mr = divide(dest, n_mr)
    dests = lax.broadcasted_iota(jnp.int32, (devices, slots), 0).astype(jnp.float32)
    counts = jnp.broadcast_to(counts.astype(jnp.float32), (8, devices)).astype(jnp.bfloat16)
    used = jnp.dot(
        counts, (dests == dest).astype(jnp.bfloat16), preferred_element_type=jnp.float32
    )
    live = (at < used[0:1]).astype(jnp.float32)
    rest, phi_base = divide(base.astype(jnp.float32), phi_dev + 1)
    psi_base, lat_base = divide(rest, lat_dev + 1)
    return jnp.concatenate(
        [
            weights[0:4] * (live * scale),
            weights[4:],
            dest_strip * phi_dev + phi_base - 2.0,
            dest_mr * lat_dev + lat_base - 2.0,
            psi_base,
            jnp.zeros_like(base, jnp.float32),
        ],
        axis=0,
    )


def lane_row():
    return lax.broadcasted_iota(jnp.int32, (1, LANES), 1).astype(jnp.float32)


def spread(values, first, each):
    index = lax.broadcasted_iota(jnp.int32, values.shape, 1) // each + first
    return jnp.take_along_axis(values, index, axis=1)


def fixed_rows(sizes, n_strip, n_mr, orders, width):
    phi_total, _, psi_count, _ = sizes

    def first_order(source):
        at, strip = divide(source, n_strip)
        core, chip = divide(at, n_mr // 2)
        _, strip = divide(n_strip - strip, n_strip)
        strip = strip.astype(jnp.int32) ^ lax.axis_index("strip")
        _, chip = divide(n_mr // 2 - chip, n_mr // 2)
        mr = (2.0 * chip + core).astype(jnp.int32) ^ lax.axis_index("mr")
        return ((strip * n_mr + mr) * orders).astype(jnp.float32)

    column = lax.broadcasted_iota(jnp.int32, (1, width), 1).astype(jnp.float32)
    at, m_there = divide(column, orders)
    source, _ = divide(at, 2)
    order = first_order(source) + m_there
    _, source = divide(lane_row(), n_strip * n_mr)
    at, m_here = divide(lane_row(), orders)
    _, part = divide(at, 2)
    return (
        first_order(source) * (1.0 / phi_total),
        m_here * (1.0 / phi_total),
        0.25 * part,
        tap_steps(order * (1.0 / phi_total)),
        tap_steps(lane_row() * (1.0 / psi_count)),
    )


def slot_weights(sizes, cols, fixed, orders, refs, here):
    _, lats, psi_count, _ = sizes
    source_turns, own_turns, quarter, phi_steps, psi_steps = fixed
    re_ref, im_ref, tail_re_ref, tail_im_ref = refs
    col = [jnp.broadcast_to(cols[:, i : i + 1], (cols.shape[0], LANES)) for i in range(15)]
    source = cos_sin_turns(col[12] * source_turns)
    own = cos_sin_turns(col[12] * own_turns + quarter)
    for tile in range(0, re_ref.shape[1], LANES):
        there = slice(tile, tile + LANES)
        first = tile // (2 * orders)
        steps = [(cos[:, there], sin[:, there]) for cos, sin in phi_steps]
        turn = times(own, [spread(x, first, 2 * orders) for x in source])
        re, im = times(turn, tap_sum(col[4:8], steps))
        re_ref[here, there] = re.astype(jnp.bfloat16)
        im_ref[here, there] = im.astype(jnp.bfloat16)
    _, r_lane = divide(lane_row(), lats)
    across = jnp.zeros_like(col[0])
    for a in range(4):
        _, row = divide(col[13] + a, lats)
        across = across + jnp.where(row == r_lane, col[a], 0.0)
    _, psi_turns = divide(col[14] * lane_row(), psi_count)
    turn = cos_sin_turns(psi_turns * (1.0 / psi_count))
    along_re, along_im = times(turn, tap_sum(col[8:12], psi_steps))
    for tile in range(0, tail_re_ref.shape[1], LANES):
        there = slice(tile, min(tile + LANES, tail_re_ref.shape[1]))
        size = there.stop - there.start
        first = tile // lats
        tail_re_ref[here, there] = (spread(along_re, first, lats) * across)[:, :size]
        tail_im_ref[here, there] = -(spread(along_im, first, lats) * across)[:, :size]


def coef_kernel(
    sizes,
    alm_hbm,
    beam_hbm,
    table_hbm,
    weights_hbm,
    base_hbm,
    counts_hbm,
    out_ref,
    re_ref,
    im_ref,
    tail_re_ref,
    tail_im_ref,
    alm,
    beam,
    table,
    weights,
    base,
    counts,
    mixed,
    rows,
    cols,
    sems,
):
    n_strip, n_mr = lax.axis_size("strip"), lax.axis_size("mr")
    orders, lanes, ells = table.shape
    k_count = beam.shape[0]
    lats = lanes // k_count
    k_pad = mixed.shape[1] // 2
    small = [(alm_hbm, alm), (beam_hbm, beam)]
    slot = [(weights_hbm, weights), (base_hbm, base), (counts_hbm, counts)]
    pairs = small + slot + [(table_hbm.at[m], table.at[m]) for m in range(orders)]
    copies = [
        pltpu.make_async_copy(source, target, sems.at[i])
        for i, (source, target) in enumerate(pairs)
    ]
    small, slot, big = copies[:2], copies[2:5], copies[5:]
    for copy in copies:
        copy.start()
    mixed[...] = jnp.zeros_like(mixed)

    fixed = fixed_rows(sizes, n_strip, n_mr, orders, re_ref.shape[1])
    for copy in slot:
        copy.wait()
    cols[...] = slot_rows(sizes, weights[...], base[...], counts[...], n_strip, n_mr).T
    block = cols.shape[0] // orders

    def mix(m):
        for c in range(2):
            product = alm[c, m, :].astype(jnp.float32)[None, :] * beam[...]
            mixed[m, c * k_pad : c * k_pad + k_count, :] = product.astype(jnp.bfloat16)

    for copy in small:
        copy.wait()
    mix(0)
    steps = [[0]] + [[m, m + 1] for m in range(1, orders - 1, 2)] + [[orders - 1]]
    for at, step in enumerate(steps):
        for m in step:
            big[m].wait()
        for m in step:
            y = lax.dot_general(mixed[m], table[m], NT, preferred_element_type=jnp.float32)
            of_row = lax.broadcasted_iota(jnp.int32, y.shape, 0) % k_pad
            of_lane = lax.broadcasted_iota(jnp.int32, y.shape, 1) // lats
            y = jnp.where(of_row == of_lane, y, 0.0)
            for c in range(2):
                total = jnp.sum(y[c * k_pad : (c + 1) * k_pad], axis=0, keepdims=True)
                rows[c * orders + m : c * orders + m + 1, :] = total
        for m in range(2 * at, min(2 * at + 2, orders)):
            here = slice(m * block, (m + 1) * block)
            slot_weights(
                sizes,
                cols[here],
                fixed,
                orders,
                (re_ref, im_ref, tail_re_ref, tail_im_ref),
                here,
            )
        for m in range(step[-1] + 1, min(step[-1] + 3, orders)):
            mix(m)
    out_ref[...] = rows[...].astype(jnp.bfloat16)


def local_part(alm, beam, wigner, base_index, interp_weights, live_counts, n_strip, n_mr):
    orders, k_count, lats, ells = wigner.shape
    k_pad = -(-k_count // 8) * 8
    lanes = k_count * lats
    slots = base_index.shape[0]
    m_total = orders * n_strip * n_mr
    width = 2 * m_total
    sizes = (2 * m_total, lats, 2 * k_count - 1, 1.0 / math.sqrt(m_total * k_count))
    base = base_index.reshape(1, slots)
    return pl.pallas_call(
        functools.partial(coef_kernel, sizes),
        out_shape=(
            jax.ShapeDtypeStruct((2 * orders, lanes), jnp.bfloat16),
            jax.ShapeDtypeStruct((slots, width), jnp.bfloat16),
            jax.ShapeDtypeStruct((slots, width), jnp.bfloat16),
            jax.ShapeDtypeStruct((slots, lanes), jnp.float32),
            jax.ShapeDtypeStruct((slots, lanes), jnp.float32),
        ),
        in_specs=[pl.BlockSpec(memory_space=pltpu.HBM)] * 6,
        out_specs=(VMEM,) * 5,
        scratch_shapes=[
            pltpu.VMEM(alm.shape, alm.dtype),
            pltpu.VMEM(beam.shape, beam.dtype),
            pltpu.VMEM((orders, lanes, ells), wigner.dtype),
            pltpu.VMEM(interp_weights.shape, interp_weights.dtype),
            pltpu.VMEM(base.shape, base.dtype),
            pltpu.VMEM(live_counts.shape, live_counts.dtype),
            pltpu.VMEM((orders, 2 * k_pad, ells), jnp.bfloat16),
            pltpu.VMEM((2 * orders, lanes), jnp.float32),
            pltpu.VMEM((slots, 16), jnp.float32),
            pltpu.SemaphoreType.DMA((orders + 5,)),
        ],
        compiler_params=pltpu.CompilerParams(vmem_limit_bytes=48 << 20),
        cost_estimate=pl.CostEstimate(
            flops=4 * wigner.size, bytes_accessed=2 * wigner.size, transcendentals=0
        ),
        name="coef",
    )(
        *(
            pltpu.with_memory_space_constraint(x, pltpu.HBM)
            for x in (
                alm,
                beam,
                wigner.reshape(orders, lanes, ells),
                interp_weights,
                base,
                live_counts,
            )
        )
    )


def sample_kernel(first, re_ref, im_ref, tail_re_ref, tail_im_ref, *refs):
    *parts, before_ref, out_ref, coef = refs
    start = 0
    for part in parts:
        coef[start : start + part.shape[0], :] = part[...]
        start += part.shape[0]
    slots, lanes = tail_re_ref.shape
    block = min(slots, 256)
    whole = lanes // LANES * LANES
    for i in range(0, slots, block):
        here = slice(i, i + block)
        both = [ref[here, first : first + start] for ref in (re_ref, im_ref)]
        both = jnp.concatenate(both, axis=0)
        both = jnp.dot(both, coef[...], preferred_element_type=jnp.float32)
        terms = both[:block] * tail_re_ref[here] + both[block:] * tail_im_ref[here]
        total = before_ref[:, here]
        if whole:
            tiles = [terms[:, j : j + LANES] for j in range(0, whole, LANES)]
            total = total + jnp.sum(sum(tiles).T, axis=0, keepdims=True)
        if whole < lanes:
            total = total + jnp.sum(terms[:, whole:].T, axis=0, keepdims=True)
        out_ref[:, here] = total


def sample(phases, first, parts, before):
    slots, lanes = phases[2].shape
    rows = sum(part.shape[0] for part in parts)
    return pl.pallas_call(
        functools.partial(sample_kernel, first),
        out_shape=jax.ShapeDtypeStruct((1, slots), jnp.float32),
        in_specs=[VMEM] * (5 + len(parts)),
        out_specs=VMEM,
        scratch_shapes=[pltpu.VMEM((rows, lanes), jnp.bfloat16)],
        compiler_params=pltpu.CompilerParams(vmem_limit_bytes=32 << 20),
        cost_estimate=pl.CostEstimate(
            flops=4 * slots * rows * lanes, bytes_accessed=1 << 20, transcendentals=0
        ),
        name="sample",
    )(*phases, *parts, before)


def on_device(alm, beam, wigner, base_index, interp_weights, live_counts):
    n_strip = lax.axis_size("strip")
    n_mr = lax.axis_size("mr")
    mine, *phases = local_part(
        alm, beam, wigner, base_index, interp_weights, live_counts, n_strip, n_mr
    )

    def swap(x, axis, d):
        return lax.ppermute(x, axis, [(i, i ^ d) for i in range(lax.axis_size(axis))])

    column = [swap(mine, "strip", d) for d in range(n_strip - 1, 0, -1)]
    column = jnp.concatenate([mine] + column, axis=0)
    plane = [column] + [swap(column, "mr", d) for d in range(n_mr - 2, 0, -2)]
    other = [swap(part, "mr", 1) for part in plane]
    parts = plane + other
    early, late = parts[:-2], parts[-2:]
    zero = jnp.zeros((1, base_index.shape[0]), jnp.float32)
    result = sample(phases, 0, early, zero)
    result = sample(phases, sum(part.shape[0] for part in early), late, result)
    return result.reshape(-1)


def solution(mesh):
    placed = (
        P(None, ("strip", "mr"), None),
        P(),
        P(("strip", "mr"), None, None, None),
        P(("strip", "mr")),
        P(None, ("strip", "mr")),
        P(("strip", "mr"), None),
    )
    return jax.shard_map(
        on_device, mesh=mesh, in_specs=placed, out_specs=P(("strip", "mr")), check_vma=False
    )
```

```python
import functools
import math

import jax
import jax.numpy as jnp
from jax import lax
from jax.experimental import pallas as pl
from jax.experimental.pallas import tpu as pltpu
from jax.sharding import PartitionSpec as P

NT = (((1,), (1,)), ((), ()))
LANES = 128
VMEM = pl.BlockSpec(memory_space=pltpu.VMEM)


def cos_sin_turns(x):
    x = x - jnp.round(x)
    u = x * x
    cos = jnp.zeros_like(x)
    sin = jnp.zeros_like(x)
    for n in range(9, -1, -1):
        cos = cos * u + (-1) ** n * (2 * math.pi) ** (2 * n) / math.factorial(2 * n)
        sin = sin * u + (-1) ** n * (2 * math.pi) ** (2 * n + 1) / math.factorial(2 * n + 1)
    return cos, sin * x


def times(x, y):
    return x[0] * y[0] - x[1] * y[1], x[1] * y[0] + x[0] * y[1]


def tap_steps(turns):
    return [cos_sin_turns(tap * turns) for tap in range(1, 4)]


def tap_sum(taps, steps):
    re = taps[0] + taps[1] * steps[0][0] + taps[2] * steps[1][0] + taps[3] * steps[2][0]
    im = taps[1] * steps[0][1] + taps[2] * steps[1][1] + taps[3] * steps[2][1]
    return re, im


def divide(x, n):
    quotient = jnp.floor((x + 0.5) * (1.0 / n))
    return quotient, x - n * quotient


def slot_rows(sizes, weights, base, counts, n_strip, n_mr):
    phi_total, lats, psi_count, scale = sizes
    slots = weights.shape[1]
    devices = n_strip * n_mr
    lat_dev, phi_dev = lats // n_mr, phi_total // n_strip
    slot = lax.broadcasted_iota(jnp.int32, (1, slots), 1).astype(jnp.float32)
    dest, at = divide(slot, slots // devices)
    dest_strip, dest_mr = divide(dest, n_mr)
    dests = lax.broadcasted_iota(jnp.int32, (devices, slots), 0).astype(jnp.float32)
    counts = jnp.broadcast_to(counts.astype(jnp.float32), (8, devices)).astype(jnp.bfloat16)
    used = jnp.dot(
        counts, (dests == dest).astype(jnp.bfloat16), preferred_element_type=jnp.float32
    )
    live = (at < used[0:1]).astype(jnp.float32)
    rest, phi_base = divide(base.astype(jnp.float32), phi_dev + 1)
    psi_base, lat_base = divide(rest, lat_dev + 1)
    return jnp.concatenate(
        [
            weights[0:4] * (live * scale),
            weights[4:],
            dest_strip * phi_dev + phi_base - 2.0,
            dest_mr * lat_dev + lat_base - 2.0,
            psi_base,
            jnp.zeros_like(base, jnp.float32),
        ],
        axis=0,
    )


def lane_row():
    return lax.broadcasted_iota(jnp.int32, (1, LANES), 1).astype(jnp.float32)


def spread(values, first, each):
    index = lax.broadcasted_iota(jnp.int32, values.shape, 1) // each + first
    return jnp.take_along_axis(values, index, axis=1)


def fixed_rows(sizes, n_strip, n_mr, orders, width):
    phi_total, _, psi_count, _ = sizes

    def first_order(source):
        at, strip = divide(source, n_strip)
        core, chip = divide(at, n_mr // 2)
        _, strip = divide(n_strip - strip, n_strip)
        _, chip = divide(n_mr // 2 - chip, n_mr // 2)
        crossed = (strip > 0.0).astype(jnp.float32) + (chip > 0.0).astype(jnp.float32)
        _, core = divide(core + crossed, 2)
        strip = strip.astype(jnp.int32) ^ lax.axis_index("strip")
        mr = (2.0 * chip + core).astype(jnp.int32) ^ lax.axis_index("mr")
        return ((strip * n_mr + mr) * orders).astype(jnp.float32)

    column = lax.broadcasted_iota(jnp.int32, (1, width), 1).astype(jnp.float32)
    at, m_there = divide(column, orders)
    source, _ = divide(at, 2)
    order = first_order(source) + m_there
    _, source = divide(lane_row(), n_strip * n_mr)
    at, m_here = divide(lane_row(), orders)
    _, part = divide(at, 2)
    return (
        first_order(source) * (1.0 / phi_total),
        m_here * (1.0 / phi_total),
        0.25 * part,
        tap_steps(order * (1.0 / phi_total)),
        tap_steps(lane_row() * (1.0 / psi_count)),
    )


def slot_weights(sizes, cols, fixed, orders, refs, here):
    _, lats, psi_count, _ = sizes
    source_turns, own_turns, quarter, phi_steps, psi_steps = fixed
    re_ref, im_ref, tail_re_ref, tail_im_ref = refs
    col = [jnp.broadcast_to(cols[:, i : i + 1], (cols.shape[0], LANES)) for i in range(15)]
    source = cos_sin_turns(col[12] * source_turns)
    own = cos_sin_turns(col[12] * own_turns + quarter)
    for tile in range(0, re_ref.shape[1], LANES):
        there = slice(tile, tile + LANES)
        first = tile // (2 * orders)
        steps = [(cos[:, there], sin[:, there]) for cos, sin in phi_steps]
        turn = times(own, [spread(x, first, 2 * orders) for x in source])
        re, im = times(turn, tap_sum(col[4:8], steps))
        re_ref[here, there] = re.astype(jnp.bfloat16)
        im_ref[here, there] = im.astype(jnp.bfloat16)
    _, r_lane = divide(lane_row(), lats)
    across = jnp.zeros_like(col[0])
    for a in range(4):
        _, row = divide(col[13] + a, lats)
        across = across + jnp.where(row == r_lane, col[a], 0.0)
    _, psi_turns = divide(col[14] * lane_row(), psi_count)
    turn = cos_sin_turns(psi_turns * (1.0 / psi_count))
    along_re, along_im = times(turn, tap_sum(col[8:12], psi_steps))
    for tile in range(0, tail_re_ref.shape[1], LANES):
        there = slice(tile, min(tile + LANES, tail_re_ref.shape[1]))
        size = there.stop - there.start
        first = tile // lats
        tail_re_ref[here, there] = (spread(along_re, first, lats) * across)[:, :size]
        tail_im_ref[here, there] = -(spread(along_im, first, lats) * across)[:, :size]


def coef_kernel(
    sizes,
    alm_hbm,
    beam_hbm,
    table_hbm,
    weights_hbm,
    base_hbm,
    counts_hbm,
    out_ref,
    re_ref,
    im_ref,
    tail_re_ref,
    tail_im_ref,
    alm,
    beam,
    table,
    weights,
    base,
    counts,
    mixed,
    rows,
    cols,
    sems,
):
    n_strip, n_mr = lax.axis_size("strip"), lax.axis_size("mr")
    orders, lanes, ells = table.shape
    k_count = beam.shape[0]
    lats = lanes // k_count
    k_pad = mixed.shape[1] // 2
    small = [(alm_hbm, alm), (beam_hbm, beam)]
    slot = [(weights_hbm, weights), (base_hbm, base), (counts_hbm, counts)]
    pairs = small + slot + [(table_hbm.at[m], table.at[m]) for m in range(orders)]
    copies = [
        pltpu.make_async_copy(source, target, sems.at[i])
        for i, (source, target) in enumerate(pairs)
    ]
    small, slot, big = copies[:2], copies[2:5], copies[5:]
    for copy in copies:
        copy.start()
    mixed[...] = jnp.zeros_like(mixed)

    fixed = fixed_rows(sizes, n_strip, n_mr, orders, re_ref.shape[1])
    for copy in slot:
        copy.wait()
    cols[...] = slot_rows(sizes, weights[...], base[...], counts[...], n_strip, n_mr).T
    block = cols.shape[0] // orders

    def mix(m):
        for c in range(2):
            product = alm[c, m, :].astype(jnp.float32)[None, :] * beam[...]
            mixed[m, c * k_pad : c * k_pad + k_count, :] = product.astype(jnp.bfloat16)

    for copy in small:
        copy.wait()
    mix(0)
    steps = [[0]] + [[m, m + 1] for m in range(1, orders - 1, 2)] + [[orders - 1]]
    for at, step in enumerate(steps):
        for m in step:
            big[m].wait()
        for m in step:
            y = lax.dot_general(mixed[m], table[m], NT, preferred_element_type=jnp.float32)
            of_row = lax.broadcasted_iota(jnp.int32, y.shape, 0) % k_pad
            of_lane = lax.broadcasted_iota(jnp.int32, y.shape, 1) // lats
            y = jnp.where(of_row == of_lane, y, 0.0)
            for c in range(2):
                total = jnp.sum(y[c * k_pad : (c + 1) * k_pad], axis=0, keepdims=True)
                rows[c * orders + m : c * orders + m + 1, :] = total
        for m in range(2 * at, min(2 * at + 2, orders)):
            here = slice(m * block, (m + 1) * block)
            slot_weights(
                sizes,
                cols[here],
                fixed,
                orders,
                (re_ref, im_ref, tail_re_ref, tail_im_ref),
                here,
            )
        for m in range(step[-1] + 1, min(step[-1] + 3, orders)):
            mix(m)
    out_ref[...] = rows[...].astype(jnp.bfloat16)


def local_part(alm, beam, wigner, base_index, interp_weights, live_counts, n_strip, n_mr):
    orders, k_count, lats, ells = wigner.shape
    k_pad = -(-k_count // 8) * 8
    lanes = k_count * lats
    slots = base_index.shape[0]
    m_total = orders * n_strip * n_mr
    width = 2 * m_total
    sizes = (2 * m_total, lats, 2 * k_count - 1, 1.0 / math.sqrt(m_total * k_count))
    base = base_index.reshape(1, slots)
    return pl.pallas_call(
        functools.partial(coef_kernel, sizes),
        out_shape=(
            jax.ShapeDtypeStruct((2 * orders, lanes), jnp.bfloat16),
            jax.ShapeDtypeStruct((slots, width), jnp.bfloat16),
            jax.ShapeDtypeStruct((slots, width), jnp.bfloat16),
            jax.ShapeDtypeStruct((slots, lanes), jnp.float32),
            jax.ShapeDtypeStruct((slots, lanes), jnp.float32),
        ),
        in_specs=[pl.BlockSpec(memory_space=pltpu.HBM)] * 6,
        out_specs=(VMEM,) * 5,
        scratch_shapes=[
            pltpu.VMEM(alm.shape, alm.dtype),
            pltpu.VMEM(beam.shape, beam.dtype),
            pltpu.VMEM((orders, lanes, ells), wigner.dtype),
            pltpu.VMEM(interp_weights.shape, interp_weights.dtype),
            pltpu.VMEM(base.shape, base.dtype),
            pltpu.VMEM(live_counts.shape, live_counts.dtype),
            pltpu.VMEM((orders, 2 * k_pad, ells), jnp.bfloat16),
            pltpu.VMEM((2 * orders, lanes), jnp.float32),
            pltpu.VMEM((slots, 16), jnp.float32),
            pltpu.SemaphoreType.DMA((orders + 5,)),
        ],
        compiler_params=pltpu.CompilerParams(vmem_limit_bytes=48 << 20),
        cost_estimate=pl.CostEstimate(
            flops=4 * wigner.size, bytes_accessed=2 * wigner.size, transcendentals=0
        ),
        name="coef",
    )(
        *(
            pltpu.with_memory_space_constraint(x, pltpu.HBM)
            for x in (
                alm,
                beam,
                wigner.reshape(orders, lanes, ells),
                interp_weights,
                base,
                live_counts,
            )
        )
    )


def sample_kernel(first, re_ref, im_ref, tail_re_ref, tail_im_ref, *refs):
    *parts, before_ref, out_ref, coef = refs
    start = 0
    for part in parts:
        coef[start : start + part.shape[0], :] = part[...]
        start += part.shape[0]
    slots, lanes = tail_re_ref.shape
    block = min(slots, 256)
    whole = lanes // LANES * LANES
    for i in range(0, slots, block):
        here = slice(i, i + block)
        both = [ref[here, first : first + start] for ref in (re_ref, im_ref)]
        both = jnp.concatenate(both, axis=0)
        both = jnp.dot(both, coef[...], preferred_element_type=jnp.float32)
        terms = both[:block] * tail_re_ref[here] + both[block:] * tail_im_ref[here]
        total = before_ref[:, here]
        if whole:
            tiles = [terms[:, j : j + LANES] for j in range(0, whole, LANES)]
            total = total + jnp.sum(sum(tiles).T, axis=0, keepdims=True)
        if whole < lanes:
            total = total + jnp.sum(terms[:, whole:].T, axis=0, keepdims=True)
        out_ref[:, here] = total


def sample(phases, first, parts, before):
    slots, lanes = phases[2].shape
    rows = sum(part.shape[0] for part in parts)
    return pl.pallas_call(
        functools.partial(sample_kernel, first),
        out_shape=jax.ShapeDtypeStruct((1, slots), jnp.float32),
        in_specs=[VMEM] * (5 + len(parts)),
        out_specs=VMEM,
        scratch_shapes=[pltpu.VMEM((rows, lanes), jnp.bfloat16)],
        compiler_params=pltpu.CompilerParams(vmem_limit_bytes=32 << 20),
        cost_estimate=pl.CostEstimate(
            flops=4 * slots * rows * lanes, bytes_accessed=1 << 20, transcendentals=0
        ),
        name="sample",
    )(*phases, *parts, before)


def on_device(alm, beam, wigner, base_index, interp_weights, live_counts):
    n_strip = lax.axis_size("strip")
    n_mr = lax.axis_size("mr")
    mine, *phases = local_part(
        alm, beam, wigner, base_index, interp_weights, live_counts, n_strip, n_mr
    )

    def swap(x, strip, mr):
        d = strip * n_mr + mr
        return lax.ppermute(x, ("strip", "mr"), [(i, i ^ d) for i in range(n_strip * n_mr)])

    column = [mine] + [swap(mine, strip, 1) for strip in range(n_strip - 1, 0, -1)]
    column = jnp.concatenate(column, axis=0)
    plane = [column] + [swap(column, 0, mr + 1) for mr in range(n_mr - 2, 0, -2)]
    other = [swap(part, 0, 1) for part in plane]
    parts = plane + other
    early, late = parts[:-2], parts[-2:]
    zero = jnp.zeros((1, base_index.shape[0]), jnp.float32)
    result = sample(phases, 0, early, zero)
    result = sample(phases, sum(part.shape[0] for part in early), late, result)
    return result.reshape(-1)


def solution(mesh):
    placed = (
        P(None, ("strip", "mr"), None),
        P(),
        P(("strip", "mr"), None, None, None),
        P(("strip", "mr")),
        P(None, ("strip", "mr")),
        P(("strip", "mr"), None),
    )
    return jax.shard_map(
        on_device, mesh=mesh, in_specs=placed, out_specs=P(("strip", "mr")), check_vma=False
    )
```

```python
import functools
import math

import jax
import jax.numpy as jnp
from jax import lax
from jax.experimental import pallas as pl
from jax.experimental.pallas import tpu as pltpu
from jax.sharding import PartitionSpec as P

NT = (((1,), (1,)), ((), ()))
LANES = 128
VMEM = pl.BlockSpec(memory_space=pltpu.VMEM)


def cos_sin_turns(x):
    x = x - jnp.round(x)
    u = x * x
    cos = jnp.zeros_like(x)
    sin = jnp.zeros_like(x)
    for n in range(9, -1, -1):
        cos = cos * u + (-1) ** n * (2 * math.pi) ** (2 * n) / math.factorial(2 * n)
        sin = sin * u + (-1) ** n * (2 * math.pi) ** (2 * n + 1) / math.factorial(2 * n + 1)
    return cos, sin * x


def times(x, y):
    return x[0] * y[0] - x[1] * y[1], x[1] * y[0] + x[0] * y[1]


def tap_steps(turns):
    return [cos_sin_turns(tap * turns) for tap in range(1, 4)]


def tap_sum(taps, steps):
    re = taps[0] + taps[1] * steps[0][0] + taps[2] * steps[1][0] + taps[3] * steps[2][0]
    im = taps[1] * steps[0][1] + taps[2] * steps[1][1] + taps[3] * steps[2][1]
    return re, im


def divide(x, n):
    quotient = jnp.floor((x + 0.5) * (1.0 / n))
    return quotient, x - n * quotient


def slot_rows(sizes, weights, base, counts, n_strip, n_mr):
    phi_total, lats, psi_count, scale = sizes
    slots = weights.shape[1]
    devices = n_strip * n_mr
    lat_dev, phi_dev = lats // n_mr, phi_total // n_strip
    slot = lax.broadcasted_iota(jnp.int32, (1, slots), 1).astype(jnp.float32)
    dest, at = divide(slot, slots // devices)
    dest_strip, dest_mr = divide(dest, n_mr)
    dests = lax.broadcasted_iota(jnp.int32, (devices, slots), 0).astype(jnp.float32)
    counts = jnp.broadcast_to(counts.astype(jnp.float32), (8, devices)).astype(jnp.bfloat16)
    used = jnp.dot(
        counts, (dests == dest).astype(jnp.bfloat16), preferred_element_type=jnp.float32
    )
    live = (at < used[0:1]).astype(jnp.float32)
    rest, phi_base = divide(base.astype(jnp.float32), phi_dev + 1)
    psi_base, lat_base = divide(rest, lat_dev + 1)
    return jnp.concatenate(
        [
            weights[0:4] * (live * scale),
            weights[4:],
            dest_strip * phi_dev + phi_base - 2.0,
            dest_mr * lat_dev + lat_base - 2.0,
            psi_base,
            jnp.zeros_like(base, jnp.float32),
        ],
        axis=0,
    )


def lane_row():
    return lax.broadcasted_iota(jnp.int32, (1, LANES), 1).astype(jnp.float32)


def spread(values, first, each):
    index = lax.broadcasted_iota(jnp.int32, values.shape, 1) // each + first
    return jnp.take_along_axis(values, index, axis=1)


def fixed_rows(sizes, n_strip, n_mr, orders, width):
    phi_total, _, psi_count, _ = sizes

    def first_order(source):
        half = n_strip // 2
        at, block = divide(source, n_strip)
        core, chip = divide(at, n_mr // 2)
        _, chip = divide(n_mr // 2 - chip, n_mr // 2)
        core = core + (chip > 0.0).astype(jnp.float32)
        own = (lax.axis_index("mr") % 2).astype(jnp.float32)
        _, sender = divide(core + own, 2)
        pair, second = divide(block - 2.0, 2)
        strip = jnp.where(block < 2.0, block * half, pair + 1.0 + sender * half)
        _, core = divide(core + jnp.where(block < 2.0, 0.0, second), 2)
        strip = strip.astype(jnp.int32) ^ lax.axis_index("strip")
        mr = (2.0 * chip + core).astype(jnp.int32) ^ lax.axis_index("mr")
        return ((strip * n_mr + mr) * orders).astype(jnp.float32)

    column = lax.broadcasted_iota(jnp.int32, (1, width), 1).astype(jnp.float32)
    at, m_there = divide(column, orders)
    source, _ = divide(at, 2)
    order = first_order(source) + m_there
    _, source = divide(lane_row(), n_strip * n_mr)
    at, m_here = divide(lane_row(), orders)
    _, part = divide(at, 2)
    return (
        first_order(source) * (1.0 / phi_total),
        m_here * (1.0 / phi_total),
        0.25 * part,
        tap_steps(order * (1.0 / phi_total)),
        tap_steps(lane_row() * (1.0 / psi_count)),
    )


def slot_weights(sizes, cols, fixed, orders, refs, here):
    _, lats, psi_count, _ = sizes
    source_turns, own_turns, quarter, phi_steps, psi_steps = fixed
    re_ref, im_ref, tail_re_ref, tail_im_ref = refs
    col = [jnp.broadcast_to(cols[:, i : i + 1], (cols.shape[0], LANES)) for i in range(15)]
    source = cos_sin_turns(col[12] * source_turns)
    own = cos_sin_turns(col[12] * own_turns + quarter)
    for tile in range(0, re_ref.shape[1], LANES):
        there = slice(tile, tile + LANES)
        first = tile // (2 * orders)
        steps = [(cos[:, there], sin[:, there]) for cos, sin in phi_steps]
        turn = times(own, [spread(x, first, 2 * orders) for x in source])
        re, im = times(turn, tap_sum(col[4:8], steps))
        re_ref[here, there] = re.astype(jnp.bfloat16)
        im_ref[here, there] = im.astype(jnp.bfloat16)
    _, r_lane = divide(lane_row(), lats)
    across = jnp.zeros_like(col[0])
    for a in range(4):
        _, row = divide(col[13] + a, lats)
        across = across + jnp.where(row == r_lane, col[a], 0.0)
    _, psi_turns = divide(col[14] * lane_row(), psi_count)
    turn = cos_sin_turns(psi_turns * (1.0 / psi_count))
    along_re, along_im = times(turn, tap_sum(col[8:12], psi_steps))
    for tile in range(0, tail_re_ref.shape[1], LANES):
        there = slice(tile, min(tile + LANES, tail_re_ref.shape[1]))
        size = there.stop - there.start
        first = tile // lats
        tail_re_ref[here, there] = (spread(along_re, first, lats) * across)[:, :size]
        tail_im_ref[here, there] = -(spread(along_im, first, lats) * across)[:, :size]


def coef_kernel(
    sizes,
    alm_hbm,
    beam_hbm,
    table_hbm,
    weights_hbm,
    base_hbm,
    counts_hbm,
    out_ref,
    re_ref,
    im_ref,
    tail_re_ref,
    tail_im_ref,
    alm,
    beam,
    table,
    weights,
    base,
    counts,
    mixed,
    rows,
    cols,
    sems,
):
    n_strip, n_mr = lax.axis_size("strip"), lax.axis_size("mr")
    orders, lanes, ells = table.shape
    k_count = beam.shape[0]
    lats = lanes // k_count
    k_pad = mixed.shape[1] // 2
    small = [(alm_hbm, alm), (beam_hbm, beam)]
    slot = [(weights_hbm, weights), (base_hbm, base), (counts_hbm, counts)]
    pairs = small + slot + [(table_hbm.at[m], table.at[m]) for m in range(orders)]
    copies = [
        pltpu.make_async_copy(source, target, sems.at[i])
        for i, (source, target) in enumerate(pairs)
    ]
    small, slot, big = copies[:2], copies[2:5], copies[5:]
    for copy in copies:
        copy.start()
    mixed[...] = jnp.zeros_like(mixed)

    fixed = fixed_rows(sizes, n_strip, n_mr, orders, re_ref.shape[1])
    for copy in slot:
        copy.wait()
    cols[...] = slot_rows(sizes, weights[...], base[...], counts[...], n_strip, n_mr).T
    block = cols.shape[0] // orders

    def mix(m):
        for c in range(2):
            product = alm[c, m, :].astype(jnp.float32)[None, :] * beam[...]
            mixed[m, c * k_pad : c * k_pad + k_count, :] = product.astype(jnp.bfloat16)

    for copy in small:
        copy.wait()
    mix(0)
    steps = [[0]] + [[m, m + 1] for m in range(1, orders - 1, 2)] + [[orders - 1]]
    for at, step in enumerate(steps):
        for m in step:
            big[m].wait()
        for m in step:
            y = lax.dot_general(mixed[m], table[m], NT, preferred_element_type=jnp.float32)
            of_row = lax.broadcasted_iota(jnp.int32, y.shape, 0) % k_pad
            of_lane = lax.broadcasted_iota(jnp.int32, y.shape, 1) // lats
            y = jnp.where(of_row == of_lane, y, 0.0)
            for c in range(2):
                total = jnp.sum(y[c * k_pad : (c + 1) * k_pad], axis=0, keepdims=True)
                rows[c * orders + m : c * orders + m + 1, :] = total
        for m in range(2 * at, min(2 * at + 2, orders)):
            here = slice(m * block, (m + 1) * block)
            slot_weights(
                sizes,
                cols[here],
                fixed,
                orders,
                (re_ref, im_ref, tail_re_ref, tail_im_ref),
                here,
            )
        for m in range(step[-1] + 1, min(step[-1] + 3, orders)):
            mix(m)
    out_ref[...] = rows[...].astype(jnp.bfloat16)


def local_part(alm, beam, wigner, base_index, interp_weights, live_counts, n_strip, n_mr):
    orders, k_count, lats, ells = wigner.shape
    k_pad = -(-k_count // 8) * 8
    lanes = k_count * lats
    slots = base_index.shape[0]
    m_total = orders * n_strip * n_mr
    width = 2 * m_total
    sizes = (2 * m_total, lats, 2 * k_count - 1, 1.0 / math.sqrt(m_total * k_count))
    base = base_index.reshape(1, slots)
    return pl.pallas_call(
        functools.partial(coef_kernel, sizes),
        out_shape=(
            jax.ShapeDtypeStruct((2 * orders, lanes), jnp.bfloat16),
            jax.ShapeDtypeStruct((slots, width), jnp.bfloat16),
            jax.ShapeDtypeStruct((slots, width), jnp.bfloat16),
            jax.ShapeDtypeStruct((slots, lanes), jnp.float32),
            jax.ShapeDtypeStruct((slots, lanes), jnp.float32),
        ),
        in_specs=[pl.BlockSpec(memory_space=pltpu.HBM)] * 6,
        out_specs=(VMEM,) * 5,
        scratch_shapes=[
            pltpu.VMEM(alm.shape, alm.dtype),
            pltpu.VMEM(beam.shape, beam.dtype),
            pltpu.VMEM((orders, lanes, ells), wigner.dtype),
            pltpu.VMEM(interp_weights.shape, interp_weights.dtype),
            pltpu.VMEM(base.shape, base.dtype),
            pltpu.VMEM(live_counts.shape, live_counts.dtype),
            pltpu.VMEM((orders, 2 * k_pad, ells), jnp.bfloat16),
            pltpu.VMEM((2 * orders, lanes), jnp.float32),
            pltpu.VMEM((slots, 16), jnp.float32),
            pltpu.SemaphoreType.DMA((orders + 5,)),
        ],
        compiler_params=pltpu.CompilerParams(vmem_limit_bytes=48 << 20),
        cost_estimate=pl.CostEstimate(
            flops=4 * wigner.size, bytes_accessed=2 * wigner.size, transcendentals=0
        ),
        name="coef",
    )(
        *(
            pltpu.with_memory_space_constraint(x, pltpu.HBM)
            for x in (
                alm,
                beam,
                wigner.reshape(orders, lanes, ells),
                interp_weights,
                base,
                live_counts,
            )
        )
    )


def sample_kernel(first, re_ref, im_ref, tail_re_ref, tail_im_ref, *refs):
    *parts, before_ref, out_ref, coef = refs
    start = 0
    for part in parts:
        coef[start : start + part.shape[0], :] = part[...]
        start += part.shape[0]
    slots, lanes = tail_re_ref.shape
    block = min(slots, 256)
    whole = lanes // LANES * LANES
    for i in range(0, slots, block):
        here = slice(i, i + block)
        both = [ref[here, first : first + start] for ref in (re_ref, im_ref)]
        both = jnp.concatenate(both, axis=0)
        both = jnp.dot(both, coef[...], preferred_element_type=jnp.float32)
        terms = both[:block] * tail_re_ref[here] + both[block:] * tail_im_ref[here]
        total = before_ref[:, here]
        if whole:
            tiles = [terms[:, j : j + LANES] for j in range(0, whole, LANES)]
            total = total + jnp.sum(sum(tiles).T, axis=0, keepdims=True)
        if whole < lanes:
            total = total + jnp.sum(terms[:, whole:].T, axis=0, keepdims=True)
        out_ref[:, here] = total


def sample(phases, first, parts, before):
    slots, lanes = phases[2].shape
    rows = sum(part.shape[0] for part in parts)
    return pl.pallas_call(
        functools.partial(sample_kernel, first),
        out_shape=jax.ShapeDtypeStruct((1, slots), jnp.float32),
        in_specs=[VMEM] * (5 + len(parts)),
        out_specs=VMEM,
        scratch_shapes=[pltpu.VMEM((rows, lanes), jnp.bfloat16)],
        compiler_params=pltpu.CompilerParams(vmem_limit_bytes=32 << 20),
        cost_estimate=pl.CostEstimate(
            flops=4 * slots * rows * lanes, bytes_accessed=1 << 20, transcendentals=0
        ),
        name="sample",
    )(*phases, *parts, before)


def on_device(alm, beam, wigner, base_index, interp_weights, live_counts):
    n_strip = lax.axis_size("strip")
    n_mr = lax.axis_size("mr")
    mine, *phases = local_part(
        alm, beam, wigner, base_index, interp_weights, live_counts, n_strip, n_mr
    )

    def swap(x, even, odd=None):
        masks = (even, even if odd is None else odd)
        pairs = [(i, i ^ masks[i % 2]) for i in range(n_strip * n_mr)]
        return lax.ppermute(x, ("strip", "mr"), pairs)

    half = n_strip // 2
    opposite = swap(mine, half * n_mr)
    pair = jnp.concatenate([mine, swap(mine, 1)], axis=0)
    column = [swap(pair, d * n_mr, (d + half) * n_mr) for d in range(1, half)]
    column = jnp.concatenate([mine, opposite] + column, axis=0)
    plane = [column] + [swap(column, mr + 1) for mr in range(n_mr - 2, 0, -2)]
    other = [swap(part, 1) for part in plane]
    parts = plane + other
    early, late = parts[:-2], parts[-2:]
    zero = jnp.zeros((1, base_index.shape[0]), jnp.float32)
    result = sample(phases, 0, early, zero)
    result = sample(phases, sum(part.shape[0] for part in early), late, result)
    return result.reshape(-1)


def solution(mesh):
    placed = (
        P(None, ("strip", "mr"), None),
        P(),
        P(("strip", "mr"), None, None, None),
        P(("strip", "mr")),
        P(None, ("strip", "mr")),
        P(("strip", "mr"), None),
    )
    return jax.shard_map(
        on_device, mesh=mesh, in_specs=placed, out_specs=P(("strip", "mr")), check_vma=False
    )
```

```python
import functools
import math

import jax
import jax.numpy as jnp
from jax import lax
from jax.experimental import pallas as pl
from jax.experimental.pallas import tpu as pltpu
from jax.sharding import PartitionSpec as P

NT = (((1,), (1,)), ((), ()))
LANES = 128
VMEM = pl.BlockSpec(memory_space=pltpu.VMEM)


def cos_sin_turns(x):
    x = x - jnp.round(x)
    u = x * x
    cos = jnp.zeros_like(x)
    sin = jnp.zeros_like(x)
    for n in range(9, -1, -1):
        cos = cos * u + (-1) ** n * (2 * math.pi) ** (2 * n) / math.factorial(2 * n)
        sin = sin * u + (-1) ** n * (2 * math.pi) ** (2 * n + 1) / math.factorial(2 * n + 1)
    return cos, sin * x


def times(x, y):
    return x[0] * y[0] - x[1] * y[1], x[1] * y[0] + x[0] * y[1]


def tap_steps(turns):
    return [cos_sin_turns(tap * turns) for tap in range(1, 4)]


def tap_sum(taps, steps):
    re = taps[0] + taps[1] * steps[0][0] + taps[2] * steps[1][0] + taps[3] * steps[2][0]
    im = taps[1] * steps[0][1] + taps[2] * steps[1][1] + taps[3] * steps[2][1]
    return re, im


def divide(x, n):
    quotient = jnp.floor((x + 0.5) * (1.0 / n))
    return quotient, x - n * quotient


def slot_rows(sizes, weights, base, counts, n_strip, n_mr):
    phi_total, lats, psi_count, scale = sizes
    slots = weights.shape[1]
    devices = n_strip * n_mr
    lat_dev, phi_dev = lats // n_mr, phi_total // n_strip
    slot = lax.broadcasted_iota(jnp.int32, (1, slots), 1).astype(jnp.float32)
    dest, at = divide(slot, slots // devices)
    dest_strip, dest_mr = divide(dest, n_mr)
    dests = lax.broadcasted_iota(jnp.int32, (devices, slots), 0).astype(jnp.float32)
    counts = jnp.broadcast_to(counts.astype(jnp.float32), (8, devices)).astype(jnp.bfloat16)
    used = jnp.dot(
        counts, (dests == dest).astype(jnp.bfloat16), preferred_element_type=jnp.float32
    )
    live = (at < used[0:1]).astype(jnp.float32)
    rest, phi_base = divide(base.astype(jnp.float32), phi_dev + 1)
    psi_base, lat_base = divide(rest, lat_dev + 1)
    return jnp.concatenate(
        [
            weights[0:4] * (live * scale),
            weights[4:],
            dest_strip * phi_dev + phi_base - 2.0,
            dest_mr * lat_dev + lat_base - 2.0,
            psi_base,
            jnp.zeros_like(base, jnp.float32),
        ],
        axis=0,
    )


def lane_row():
    return lax.broadcasted_iota(jnp.int32, (1, LANES), 1).astype(jnp.float32)


def spread(values, first, each):
    index = lax.broadcasted_iota(jnp.int32, values.shape, 1) // each + first
    return jnp.take_along_axis(values, index, axis=1)


def fixed_rows(sizes, n_strip, n_mr, orders, width):
    phi_total, _, psi_count, _ = sizes

    def first_order(source):
        half = n_strip // 2
        at, block = divide(source, n_strip)
        core, chip = divide(at, n_mr // 2)
        _, chip = divide(n_mr // 2 - chip, n_mr // 2)
        core = core + (chip > 0.0).astype(jnp.float32)
        own = (lax.axis_index("mr") % 2).astype(jnp.float32)
        _, sender = divide(core + own, 2)
        pair, second = divide(block - 2.0, 2)
        strip = jnp.where(block < 2.0, block * half, pair + 1.0 + sender * half)
        _, core = divide(core + jnp.where(block < 2.0, 0.0, second), 2)
        strip = strip.astype(jnp.int32) ^ lax.axis_index("strip")
        mr = (2.0 * chip + core).astype(jnp.int32) ^ lax.axis_index("mr")
        return ((strip * n_mr + mr) * orders).astype(jnp.float32)

    column = lax.broadcasted_iota(jnp.int32, (1, width), 1).astype(jnp.float32)
    at, m_there = divide(column, orders)
    source, _ = divide(at, 2)
    order = first_order(source) + m_there
    _, source = divide(lane_row(), n_strip * n_mr)
    at, m_here = divide(lane_row(), orders)
    _, part = divide(at, 2)
    return (
        first_order(source) * (1.0 / phi_total),
        m_here * (1.0 / phi_total),
        0.25 * part,
        tap_steps(order * (1.0 / phi_total)),
        tap_steps(lane_row() * (1.0 / psi_count)),
    )


def slot_weights(sizes, cols, fixed, orders, refs, here):
    _, lats, psi_count, _ = sizes
    source_turns, own_turns, quarter, phi_steps, psi_steps = fixed
    re_ref, im_ref, tail_re_ref, tail_im_ref = refs
    col = [jnp.broadcast_to(cols[:, i : i + 1], (cols.shape[0], LANES)) for i in range(15)]
    source = cos_sin_turns(col[12] * source_turns)
    own = cos_sin_turns(col[12] * own_turns + quarter)
    for tile in range(0, re_ref.shape[1], LANES):
        there = slice(tile, tile + LANES)
        first = tile // (2 * orders)
        steps = [(cos[:, there], sin[:, there]) for cos, sin in phi_steps]
        turn = times(own, [spread(x, first, 2 * orders) for x in source])
        re, im = times(turn, tap_sum(col[4:8], steps))
        re_ref[here, there] = re.astype(jnp.bfloat16)
        im_ref[here, there] = im.astype(jnp.bfloat16)
    _, r_lane = divide(lane_row(), lats)
    across = jnp.zeros_like(col[0])
    for a in range(4):
        _, row = divide(col[13] + a, lats)
        across = across + jnp.where(row == r_lane, col[a], 0.0)
    _, psi_turns = divide(col[14] * lane_row(), psi_count)
    turn = cos_sin_turns(psi_turns * (1.0 / psi_count))
    along_re, along_im = times(turn, tap_sum(col[8:12], psi_steps))
    for tile in range(0, tail_re_ref.shape[1], LANES):
        there = slice(tile, min(tile + LANES, tail_re_ref.shape[1]))
        size = there.stop - there.start
        first = tile // lats
        tail_re_ref[here, there] = (spread(along_re, first, lats) * across)[:, :size]
        tail_im_ref[here, there] = -(spread(along_im, first, lats) * across)[:, :size]


def coef_kernel(
    sizes,
    alm_hbm,
    beam_hbm,
    table_hbm,
    weights_hbm,
    base_hbm,
    counts_hbm,
    out_ref,
    re_ref,
    im_ref,
    tail_re_ref,
    tail_im_ref,
    alm,
    beam,
    table,
    weights,
    base,
    counts,
    mixed,
    rows,
    cols,
    sems,
):
    n_strip, n_mr = lax.axis_size("strip"), lax.axis_size("mr")
    orders, lanes, ells = table.shape
    k_count = beam.shape[0]
    lats = lanes // k_count
    k_pad = mixed.shape[1] // 2
    small = [(alm_hbm, alm), (beam_hbm, beam)]
    slot = [(weights_hbm, weights), (base_hbm, base), (counts_hbm, counts)]
    pairs = small + slot + [(table_hbm.at[m], table.at[m]) for m in range(orders)]
    copies = [
        pltpu.make_async_copy(source, target, sems.at[i])
        for i, (source, target) in enumerate(pairs)
    ]
    small, slot, big = copies[:2], copies[2:5], copies[5:]
    for copy in big[:1] + small + slot + big[1:]:
        copy.start()
    whole = k_count // 8 * 8
    if whole < k_pad:
        for m in range(orders):
            for c in range(2):
                padded = slice(c * k_pad + whole, (c + 1) * k_pad)
                mixed[m, padded, :] = jnp.zeros((k_pad - whole, ells), jnp.bfloat16)

    fixed = fixed_rows(sizes, n_strip, n_mr, orders, re_ref.shape[1])
    for copy in slot:
        copy.wait()
    cols[...] = slot_rows(sizes, weights[...], base[...], counts[...], n_strip, n_mr).T
    block = cols.shape[0] // orders

    def mix(m):
        for c in range(2):
            product = alm[c, m, :].astype(jnp.float32)[None, :] * beam[...]
            mixed[m, c * k_pad : c * k_pad + k_count, :] = product.astype(jnp.bfloat16)

    for copy in small:
        copy.wait()
    mix(0)
    steps = [[0]] + [[m, m + 1] for m in range(1, orders - 1, 2)] + [[orders - 1]]
    for at, step in enumerate(steps):
        for m in step:
            big[m].wait()
        for m in step:
            y = lax.dot_general(mixed[m], table[m], NT, preferred_element_type=jnp.float32)
            of_row = lax.broadcasted_iota(jnp.int32, y.shape, 0) % k_pad
            of_lane = lax.broadcasted_iota(jnp.int32, y.shape, 1) // lats
            y = jnp.where(of_row == of_lane, y, 0.0)
            for c in range(2):
                total = jnp.sum(y[c * k_pad : (c + 1) * k_pad], axis=0, keepdims=True)
                rows[c * orders + m : c * orders + m + 1, :] = total
        for m in range(2 * at, min(2 * at + 2, orders)):
            here = slice(m * block, (m + 1) * block)
            slot_weights(
                sizes,
                cols[here],
                fixed,
                orders,
                (re_ref, im_ref, tail_re_ref, tail_im_ref),
                here,
            )
        for m in range(step[-1] + 1, min(step[-1] + 3, orders)):
            mix(m)
    out_ref[...] = rows[...].astype(jnp.bfloat16)


def local_part(alm, beam, wigner, base_index, interp_weights, live_counts, n_strip, n_mr):
    orders, k_count, lats, ells = wigner.shape
    k_pad = -(-k_count // 8) * 8
    lanes = k_count * lats
    slots = base_index.shape[0]
    m_total = orders * n_strip * n_mr
    width = 2 * m_total
    sizes = (2 * m_total, lats, 2 * k_count - 1, 1.0 / math.sqrt(m_total * k_count))
    base = base_index.reshape(1, slots)
    return pl.pallas_call(
        functools.partial(coef_kernel, sizes),
        out_shape=(
            jax.ShapeDtypeStruct((2 * orders, lanes), jnp.bfloat16),
            jax.ShapeDtypeStruct((slots, width), jnp.bfloat16),
            jax.ShapeDtypeStruct((slots, width), jnp.bfloat16),
            jax.ShapeDtypeStruct((slots, lanes), jnp.float32),
            jax.ShapeDtypeStruct((slots, lanes), jnp.float32),
        ),
        in_specs=[pl.BlockSpec(memory_space=pltpu.HBM)] * 6,
        out_specs=(VMEM,) * 5,
        scratch_shapes=[
            pltpu.VMEM(alm.shape, alm.dtype),
            pltpu.VMEM(beam.shape, beam.dtype),
            pltpu.VMEM((orders, lanes, ells), wigner.dtype),
            pltpu.VMEM(interp_weights.shape, interp_weights.dtype),
            pltpu.VMEM(base.shape, base.dtype),
            pltpu.VMEM(live_counts.shape, live_counts.dtype),
            pltpu.VMEM((orders, 2 * k_pad, ells), jnp.bfloat16),
            pltpu.VMEM((2 * orders, lanes), jnp.float32),
            pltpu.VMEM((slots, 16), jnp.float32),
            pltpu.SemaphoreType.DMA((orders + 5,)),
        ],
        compiler_params=pltpu.CompilerParams(vmem_limit_bytes=48 << 20),
        cost_estimate=pl.CostEstimate(
            flops=4 * wigner.size, bytes_accessed=2 * wigner.size, transcendentals=0
        ),
        name="coef",
    )(
        *(
            pltpu.with_memory_space_constraint(x, pltpu.HBM)
            for x in (
                alm,
                beam,
                wigner.reshape(orders, lanes, ells),
                interp_weights,
                base,
                live_counts,
            )
        )
    )


def sample_kernel(first, re_ref, im_ref, tail_re_ref, tail_im_ref, *refs):
    *parts, before_ref, out_ref, coef = refs
    start = 0
    for part in parts:
        coef[start : start + part.shape[0], :] = part[...]
        start += part.shape[0]
    slots, lanes = tail_re_ref.shape
    block = min(slots, 256)
    whole = lanes // LANES * LANES
    for i in range(0, slots, block):
        here = slice(i, i + block)
        both = [ref[here, first : first + start] for ref in (re_ref, im_ref)]
        both = jnp.concatenate(both, axis=0)
        both = jnp.dot(both, coef[...], preferred_element_type=jnp.float32)
        terms = both[:block] * tail_re_ref[here] + both[block:] * tail_im_ref[here]
        total = before_ref[:, here]
        if whole:
            tiles = [terms[:, j : j + LANES] for j in range(0, whole, LANES)]
            total = total + jnp.sum(sum(tiles).T, axis=0, keepdims=True)
        if whole < lanes:
            total = total + jnp.sum(terms[:, whole:].T, axis=0, keepdims=True)
        out_ref[:, here] = total


def sample(phases, first, parts, before):
    slots, lanes = phases[2].shape
    rows = sum(part.shape[0] for part in parts)
    return pl.pallas_call(
        functools.partial(sample_kernel, first),
        out_shape=jax.ShapeDtypeStruct((1, slots), jnp.float32),
        in_specs=[VMEM] * (5 + len(parts)),
        out_specs=VMEM,
        scratch_shapes=[pltpu.VMEM((rows, lanes), jnp.bfloat16)],
        compiler_params=pltpu.CompilerParams(vmem_limit_bytes=32 << 20),
        cost_estimate=pl.CostEstimate(
            flops=4 * slots * rows * lanes, bytes_accessed=1 << 20, transcendentals=0
        ),
        name="sample",
    )(*phases, *parts, before)


def on_device(alm, beam, wigner, base_index, interp_weights, live_counts):
    n_strip = lax.axis_size("strip")
    n_mr = lax.axis_size("mr")
    mine, *phases = local_part(
        alm, beam, wigner, base_index, interp_weights, live_counts, n_strip, n_mr
    )

    def swap(x, even, odd=None):
        masks = (even, even if odd is None else odd)
        pairs = [(i, i ^ masks[i % 2]) for i in range(n_strip * n_mr)]
        return lax.ppermute(x, ("strip", "mr"), pairs)

    half = n_strip // 2
    opposite = swap(mine, half * n_mr)
    pair = jnp.concatenate([mine, swap(mine, 1)], axis=0)
    column = [swap(pair, d * n_mr, (d + half) * n_mr) for d in range(1, half)]
    column = jnp.concatenate([mine, opposite] + column, axis=0)
    plane = [column] + [swap(column, mr + 1) for mr in range(n_mr - 2, 0, -2)]
    other = [swap(part, 1) for part in plane]
    parts = plane + other
    early, late = parts[:-2], parts[-2:]
    zero = jnp.zeros((1, base_index.shape[0]), jnp.float32)
    result = sample(phases, 0, early, zero)
    result = sample(phases, sum(part.shape[0] for part in early), late, result)
    return result.reshape(-1)


def solution(mesh):
    placed = (
        P(None, ("strip", "mr"), None),
        P(),
        P(("strip", "mr"), None, None, None),
        P(("strip", "mr")),
        P(None, ("strip", "mr")),
        P(("strip", "mr"), None),
    )
    return jax.shard_map(
        on_device, mesh=mesh, in_specs=placed, out_specs=P(("strip", "mr")), check_vma=False
    )
```

```python
import functools
import math

import jax
import jax.numpy as jnp
from jax import lax
from jax.experimental import pallas as pl
from jax.experimental.pallas import tpu as pltpu
from jax.sharding import PartitionSpec as P

NT = (((1,), (1,)), ((), ()))
LANES = 128
VMEM = pl.BlockSpec(memory_space=pltpu.VMEM)


def cos_sin_turns(x):
    x = x - jnp.round(x)
    u = x * x
    cos = jnp.zeros_like(x)
    sin = jnp.zeros_like(x)
    for n in range(9, -1, -1):
        cos = cos * u + (-1) ** n * (2 * math.pi) ** (2 * n) / math.factorial(2 * n)
        if n < 9:
            sin = sin * u + (-1) ** n * (2 * math.pi) ** (2 * n + 1) / math.factorial(2 * n + 1)
    return cos, sin * x


def times(x, y):
    return x[0] * y[0] - x[1] * y[1], x[1] * y[0] + x[0] * y[1]


def tap_steps(turns):
    return [cos_sin_turns(tap * turns) for tap in range(1, 4)]


def tap_sum(taps, steps):
    re = taps[0] + taps[1] * steps[0][0] + taps[2] * steps[1][0] + taps[3] * steps[2][0]
    im = taps[1] * steps[0][1] + taps[2] * steps[1][1] + taps[3] * steps[2][1]
    return re, im


def divide(x, n):
    quotient = jnp.floor((x + 0.5) * (1.0 / n))
    return quotient, x - n * quotient


def slot_rows(sizes, weights, base, counts, n_strip, n_mr):
    phi_total, lats, psi_count, scale = sizes
    slots = weights.shape[1]
    devices = n_strip * n_mr
    lat_dev, phi_dev = lats // n_mr, phi_total // n_strip
    slot = lax.broadcasted_iota(jnp.int32, (1, slots), 1).astype(jnp.float32)
    dest, at = divide(slot, slots // devices)
    dest_strip, dest_mr = divide(dest, n_mr)
    dests = lax.broadcasted_iota(jnp.int32, (devices, slots), 0).astype(jnp.float32)
    counts = jnp.broadcast_to(counts.astype(jnp.float32), (8, devices)).astype(jnp.bfloat16)
    used = jnp.dot(
        counts, (dests == dest).astype(jnp.bfloat16), preferred_element_type=jnp.float32
    )
    live = (at < used[0:1]).astype(jnp.float32)
    rest, phi_base = divide(base.astype(jnp.float32), phi_dev + 1)
    psi_base, lat_base = divide(rest, lat_dev + 1)
    return jnp.concatenate(
        [
            weights[0:4] * (live * scale),
            weights[4:],
            dest_strip * phi_dev + phi_base - 2.0,
            dest_mr * lat_dev + lat_base - 2.0,
            psi_base,
            jnp.zeros_like(base, jnp.float32),
        ],
        axis=0,
    )


def lane_row():
    return lax.broadcasted_iota(jnp.int32, (1, LANES), 1).astype(jnp.float32)


def spread(values, first, each):
    index = lax.broadcasted_iota(jnp.int32, values.shape, 1) // each + first
    return jnp.take_along_axis(values, index, axis=1)


def fixed_rows(sizes, n_strip, n_mr, orders, width):
    phi_total, _, psi_count, _ = sizes

    def first_order(source):
        half = n_strip // 2
        at, block = divide(source, n_strip)
        core, chip = divide(at, n_mr // 2)
        _, chip = divide(n_mr // 2 - chip, n_mr // 2)
        core = core + (chip > 0.0).astype(jnp.float32)
        own = (lax.axis_index("mr") % 2).astype(jnp.float32)
        _, sender = divide(core + own, 2)
        pair, second = divide(block - 2.0, 2)
        strip = jnp.where(block < 2.0, block * half, pair + 1.0 + sender * half)
        _, core = divide(core + jnp.where(block < 2.0, 0.0, second), 2)
        strip = strip.astype(jnp.int32) ^ lax.axis_index("strip")
        mr = (2.0 * chip + core).astype(jnp.int32) ^ lax.axis_index("mr")
        return ((strip * n_mr + mr) * orders).astype(jnp.float32)

    column = lax.broadcasted_iota(jnp.int32, (1, width), 1).astype(jnp.float32)
    at, m_there = divide(column, orders)
    source, _ = divide(at, 2)
    order = first_order(source) + m_there
    _, source = divide(lane_row(), n_strip * n_mr)
    at, m_here = divide(lane_row(), orders)
    _, part = divide(at, 2)
    return (
        first_order(source) * (1.0 / phi_total),
        m_here * (1.0 / phi_total),
        0.25 * part,
        tap_steps(order * (1.0 / phi_total)),
        tap_steps(lane_row() * (1.0 / psi_count)),
    )


def slot_weights(sizes, cols, fixed, orders, refs, here):
    _, lats, psi_count, _ = sizes
    source_turns, own_turns, quarter, phi_steps, psi_steps = fixed
    re_ref, im_ref, tail_re_ref, tail_im_ref = refs
    col = [jnp.broadcast_to(cols[:, i : i + 1], (cols.shape[0], LANES)) for i in range(15)]
    source = cos_sin_turns(col[12] * source_turns)
    own = cos_sin_turns(col[12] * own_turns + quarter)
    for tile in range(0, re_ref.shape[1], LANES):
        there = slice(tile, tile + LANES)
        first = tile // (2 * orders)
        steps = [(cos[:, there], sin[:, there]) for cos, sin in phi_steps]
        turn = times(own, [spread(x, first, 2 * orders) for x in source])
        re, im = times(turn, tap_sum(col[4:8], steps))
        re_ref[here, there] = re.astype(jnp.bfloat16)
        im_ref[here, there] = im.astype(jnp.bfloat16)
    _, r_lane = divide(lane_row(), lats)
    across = jnp.zeros_like(col[0])
    for a in range(4):
        _, row = divide(col[13] + a, lats)
        across = across + jnp.where(row == r_lane, col[a], 0.0)
    _, psi_turns = divide(col[14] * lane_row(), psi_count)
    turn = cos_sin_turns(psi_turns * (1.0 / psi_count))
    along_re, along_im = times(turn, tap_sum(col[8:12], psi_steps))
    for tile in range(0, tail_re_ref.shape[1], LANES):
        there = slice(tile, min(tile + LANES, tail_re_ref.shape[1]))
        size = there.stop - there.start
        first = tile // lats
        tail_re_ref[here, there] = (spread(along_re, first, lats) * across)[:, :size]
        tail_im_ref[here, there] = -(spread(along_im, first, lats) * across)[:, :size]


def coef_kernel(
    sizes,
    alm_hbm,
    beam_hbm,
    table_hbm,
    weights_hbm,
    base_hbm,
    counts_hbm,
    out_ref,
    re_ref,
    im_ref,
    tail_re_ref,
    tail_im_ref,
    alm,
    beam,
    table,
    weights,
    base,
    counts,
    mixed,
    rows,
    cols,
    sems,
):
    n_strip, n_mr = lax.axis_size("strip"), lax.axis_size("mr")
    orders, lanes, ells = table.shape
    k_count = beam.shape[0]
    lats = lanes // k_count
    k_pad = mixed.shape[1] // 2
    small = [(alm_hbm, alm), (beam_hbm, beam)]
    slot = [(weights_hbm, weights), (base_hbm, base), (counts_hbm, counts)]
    pairs = small + slot + [(table_hbm.at[m], table.at[m]) for m in range(orders)]
    copies = [
        pltpu.make_async_copy(source, target, sems.at[i])
        for i, (source, target) in enumerate(pairs)
    ]
    small, slot, big = copies[:2], copies[2:5], copies[5:]
    for copy in big[:1] + small + slot + big[1:]:
        copy.start()
    mixed[...] = jnp.zeros_like(mixed)

    fixed = fixed_rows(sizes, n_strip, n_mr, orders, re_ref.shape[1])
    for copy in slot:
        copy.wait()
    cols[...] = slot_rows(sizes, weights[...], base[...], counts[...], n_strip, n_mr).T
    block = cols.shape[0] // orders

    def mix(m):
        for c in range(2):
            product = alm[c, m, :].astype(jnp.float32)[None, :] * beam[...]
            mixed[m, c * k_pad : c * k_pad + k_count, :] = product.astype(jnp.bfloat16)

    for copy in small:
        copy.wait()
    mix(0)
    steps = [[0]] + [[m, m + 1] for m in range(1, orders - 1, 2)] + [[orders - 1]]
    for at, step in enumerate(steps):
        for m in step:
            big[m].wait()
        for m in step:
            y = lax.dot_general(mixed[m], table[m], NT, preferred_element_type=jnp.float32)
            of_row = lax.broadcasted_iota(jnp.int32, y.shape, 0) % k_pad
            of_lane = lax.broadcasted_iota(jnp.int32, y.shape, 1) // lats
            y = jnp.where(of_row == of_lane, y, 0.0)
            for c in range(2):
                total = jnp.sum(y[c * k_pad : (c + 1) * k_pad], axis=0, keepdims=True)
                rows[c * orders + m : c * orders + m + 1, :] = total
        for m in range(2 * at, min(2 * at + 2, orders)):
            here = slice(m * block, (m + 1) * block)
            slot_weights(
                sizes,
                cols[here],
                fixed,
                orders,
                (re_ref, im_ref, tail_re_ref, tail_im_ref),
                here,
            )
        for m in range(step[-1] + 1, min(step[-1] + 3, orders)):
            mix(m)
    out_ref[...] = rows[...].astype(jnp.bfloat16)


def local_part(alm, beam, wigner, base_index, interp_weights, live_counts, n_strip, n_mr):
    orders, k_count, lats, ells = wigner.shape
    k_pad = -(-k_count // 8) * 8
    lanes = k_count * lats
    slots = base_index.shape[0]
    m_total = orders * n_strip * n_mr
    width = 2 * m_total
    sizes = (2 * m_total, lats, 2 * k_count - 1, 1.0 / math.sqrt(m_total * k_count))
    base = base_index.reshape(1, slots)
    return pl.pallas_call(
        functools.partial(coef_kernel, sizes),
        out_shape=(
            jax.ShapeDtypeStruct((2 * orders, lanes), jnp.bfloat16),
            jax.ShapeDtypeStruct((slots, width), jnp.bfloat16),
            jax.ShapeDtypeStruct((slots, width), jnp.bfloat16),
            jax.ShapeDtypeStruct((slots, lanes), jnp.float32),
            jax.ShapeDtypeStruct((slots, lanes), jnp.float32),
        ),
        in_specs=[pl.BlockSpec(memory_space=pltpu.HBM)] * 6,
        out_specs=(VMEM,) * 5,
        scratch_shapes=[
            pltpu.VMEM(alm.shape, alm.dtype),
            pltpu.VMEM(beam.shape, beam.dtype),
            pltpu.VMEM((orders, lanes, ells), wigner.dtype),
            pltpu.VMEM(interp_weights.shape, interp_weights.dtype),
            pltpu.VMEM(base.shape, base.dtype),
            pltpu.VMEM(live_counts.shape, live_counts.dtype),
            pltpu.VMEM((orders, 2 * k_pad, ells), jnp.bfloat16),
            pltpu.VMEM((2 * orders, lanes), jnp.float32),
            pltpu.VMEM((slots, 16), jnp.float32),
            pltpu.SemaphoreType.DMA((orders + 5,)),
        ],
        compiler_params=pltpu.CompilerParams(vmem_limit_bytes=48 << 20),
        cost_estimate=pl.CostEstimate(
            flops=4 * wigner.size, bytes_accessed=2 * wigner.size, transcendentals=0
        ),
        name="coef",
    )(
        *(
            pltpu.with_memory_space_constraint(x, pltpu.HBM)
            for x in (
                alm,
                beam,
                wigner.reshape(orders, lanes, ells),
                interp_weights,
                base,
                live_counts,
            )
        )
    )


def sample_kernel(first, re_ref, im_ref, tail_re_ref, tail_im_ref, *refs):
    *parts, before_ref, out_ref, coef = refs
    start = 0
    for part in parts:
        coef[start : start + part.shape[0], :] = part[...]
        start += part.shape[0]
    slots, lanes = tail_re_ref.shape
    block = min(slots, 256)
    whole = lanes // LANES * LANES
    for i in range(0, slots, block):
        here = slice(i, i + block)
        both = [ref[here, first : first + start] for ref in (re_ref, im_ref)]
        both = jnp.concatenate(both, axis=0)
        both = jnp.dot(both, coef[...], preferred_element_type=jnp.float32)
        terms = both[:block] * tail_re_ref[here] + both[block:] * tail_im_ref[here]
        total = before_ref[:, here]
        if whole:
            tiles = [terms[:, j : j + LANES] for j in range(0, whole, LANES)]
            total = total + jnp.sum(sum(tiles).T, axis=0, keepdims=True)
        if whole < lanes:
            total = total + jnp.sum(terms[:, whole:].T, axis=0, keepdims=True)
        out_ref[:, here] = total


def sample(phases, first, parts, before):
    slots, lanes = phases[2].shape
    rows = sum(part.shape[0] for part in parts)
    return pl.pallas_call(
        functools.partial(sample_kernel, first),
        out_shape=jax.ShapeDtypeStruct((1, slots), jnp.float32),
        in_specs=[VMEM] * (5 + len(parts)),
        out_specs=VMEM,
        scratch_shapes=[pltpu.VMEM((rows, lanes), jnp.bfloat16)],
        compiler_params=pltpu.CompilerParams(vmem_limit_bytes=32 << 20),
        cost_estimate=pl.CostEstimate(
            flops=4 * slots * rows * lanes, bytes_accessed=1 << 20, transcendentals=0
        ),
        name="sample",
    )(*phases, *parts, before)


def on_device(alm, beam, wigner, base_index, interp_weights, live_counts):
    n_strip = lax.axis_size("strip")
    n_mr = lax.axis_size("mr")
    mine, *phases = local_part(
        alm, beam, wigner, base_index, interp_weights, live_counts, n_strip, n_mr
    )

    def swap(x, even, odd=None):
        masks = (even, even if odd is None else odd)
        pairs = [(i, i ^ masks[i % 2]) for i in range(n_strip * n_mr)]
        return lax.ppermute(x, ("strip", "mr"), pairs)

    half = n_strip // 2
    opposite = swap(mine, half * n_mr)
    pair = jnp.concatenate([mine, swap(mine, 1)], axis=0)
    column = [swap(pair, d * n_mr, (d + half) * n_mr) for d in range(1, half)]
    column = jnp.concatenate([mine, opposite] + column, axis=0)
    plane = [column] + [swap(column, mr + 1) for mr in range(n_mr - 2, 0, -2)]
    other = [swap(part, 1) for part in plane]
    parts = plane + other
    early, late = parts[:-2], parts[-2:]
    zero = jnp.zeros((1, base_index.shape[0]), jnp.float32)
    result = sample(phases, 0, early, zero)
    result = sample(phases, sum(part.shape[0] for part in early), late, result)
    return result.reshape(-1)


def solution(mesh):
    placed = (
        P(None, ("strip", "mr"), None),
        P(),
        P(("strip", "mr"), None, None, None),
        P(("strip", "mr")),
        P(None, ("strip", "mr")),
        P(("strip", "mr"), None),
    )
    return jax.shard_map(
        on_device, mesh=mesh, in_specs=placed, out_specs=P(("strip", "mr")), check_vma=False
    )
```

```python
import functools
import math

import jax
import jax.numpy as jnp
from jax import lax
from jax.experimental import pallas as pl
from jax.experimental.pallas import tpu as pltpu
from jax.sharding import PartitionSpec as P

NT = (((1,), (1,)), ((), ()))
LANES = 128
VMEM = pl.BlockSpec(memory_space=pltpu.VMEM)


def cos_sin_turns(x):
    x = x - jnp.round(x)
    u = x * x
    cos = jnp.zeros_like(x)
    sin = jnp.zeros_like(x)
    for n in range(9, -1, -1):
        cos = cos * u + (-1) ** n * (2 * math.pi) ** (2 * n) / math.factorial(2 * n)
        sin = sin * u + (-1) ** n * (2 * math.pi) ** (2 * n + 1) / math.factorial(2 * n + 1)
    return cos, sin * x


def times(x, y):
    return x[0] * y[0] - x[1] * y[1], x[1] * y[0] + x[0] * y[1]


def tap_steps(turns):
    return [cos_sin_turns(tap * turns) for tap in range(1, 4)]


def tap_sum(taps, steps):
    re = taps[0] + taps[1] * steps[0][0] + taps[2] * steps[1][0] + taps[3] * steps[2][0]
    im = taps[1] * steps[0][1] + taps[2] * steps[1][1] + taps[3] * steps[2][1]
    return re, im


def divide(x, n):
    quotient = jnp.floor((x + 0.5) * (1.0 / n))
    return quotient, x - n * quotient


def slot_rows(sizes, weights, base, counts, n_strip, n_mr):
    phi_total, lats, psi_count, scale = sizes
    slots = weights.shape[1]
    devices = n_strip * n_mr
    lat_dev, phi_dev = lats // n_mr, phi_total // n_strip
    slot = lax.broadcasted_iota(jnp.int32, (1, slots), 1).astype(jnp.float32)
    dest, at = divide(slot, slots // devices)
    dest_strip, dest_mr = divide(dest, n_mr)
    dests = lax.broadcasted_iota(jnp.int32, (devices, slots), 0).astype(jnp.float32)
    counts = jnp.broadcast_to(counts.astype(jnp.float32), (8, devices)).astype(jnp.bfloat16)
    used = jnp.dot(
        counts, (dests == dest).astype(jnp.bfloat16), preferred_element_type=jnp.float32
    )
    live = (at < used[0:1]).astype(jnp.float32)
    rest, phi_base = divide(base.astype(jnp.float32), phi_dev + 1)
    psi_base, lat_base = divide(rest, lat_dev + 1)
    return jnp.concatenate(
        [
            weights[0:4] * (live * scale),
            weights[4:],
            dest_strip * phi_dev + phi_base - 2.0,
            dest_mr * lat_dev + lat_base - 2.0,
            psi_base,
            jnp.zeros_like(base, jnp.float32),
        ],
        axis=0,
    )


def lane_row():
    return lax.broadcasted_iota(jnp.int32, (1, LANES), 1).astype(jnp.float32)


def spread(values, first, each):
    index = lax.broadcasted_iota(jnp.int32, values.shape, 1) // each + first
    return jnp.take_along_axis(values, index, axis=1)


def fixed_rows(sizes, n_strip, n_mr, orders, width):
    phi_total, _, psi_count, _ = sizes

    def first_order(source):
        half = n_strip // 2
        at, block = divide(source, n_strip)
        core, chip = divide(at, n_mr // 2)
        _, chip = divide(n_mr // 2 - chip, n_mr // 2)
        core = core + (chip > 0.0).astype(jnp.float32)
        own = (lax.axis_index("mr") % 2).astype(jnp.float32)
        _, sender = divide(core + own, 2)
        pair, second = divide(block - 2.0, 2)
        strip = jnp.where(block < 2.0, block * half, pair + 1.0 + sender * half)
        _, core = divide(core + jnp.where(block < 2.0, 0.0, second), 2)
        strip = strip.astype(jnp.int32) ^ lax.axis_index("strip")
        mr = (2.0 * chip + core).astype(jnp.int32) ^ lax.axis_index("mr")
        return ((strip * n_mr + mr) * orders).astype(jnp.float32)

    column = lax.broadcasted_iota(jnp.int32, (1, width), 1).astype(jnp.float32)
    at, m_there = divide(column, orders)
    source, _ = divide(at, 2)
    order = first_order(source) + m_there
    _, source = divide(lane_row(), n_strip * n_mr)
    at, m_here = divide(lane_row(), orders)
    _, part = divide(at, 2)
    return (
        first_order(source) * (1.0 / phi_total),
        m_here * (1.0 / phi_total),
        0.25 * part,
        tap_steps(order * (1.0 / phi_total)),
        tap_steps(lane_row() * (1.0 / psi_count)),
    )


def slot_weights(sizes, cols, fixed, orders, refs, here):
    _, lats, psi_count, _ = sizes
    source_turns, own_turns, quarter, phi_steps, psi_steps = fixed
    re_ref, im_ref, tail_re_ref, tail_im_ref = refs
    col = [jnp.broadcast_to(cols[:, i : i + 1], (cols.shape[0], LANES)) for i in range(15)]
    source = cos_sin_turns(col[12] * source_turns)
    own = cos_sin_turns(col[12] * own_turns + quarter)
    for tile in range(0, re_ref.shape[1], LANES):
        there = slice(tile, tile + LANES)
        first = tile // (2 * orders)
        steps = [(cos[:, there], sin[:, there]) for cos, sin in phi_steps]
        turn = times(own, [spread(x, first, 2 * orders) for x in source])
        re, im = times(turn, tap_sum(col[4:8], steps))
        re_ref[here, there] = re.astype(jnp.bfloat16)
        im_ref[here, there] = im.astype(jnp.bfloat16)
    _, r_lane = divide(lane_row(), lats)
    across = jnp.zeros_like(col[0])
    _, tap = divide(r_lane - col[13], lats)
    for a in range(4):
        across = across + jnp.where(tap == a, col[a], 0.0)
    _, psi_turns = divide(col[14] * lane_row(), psi_count)
    turn = cos_sin_turns(psi_turns * (1.0 / psi_count))
    along_re, along_im = times(turn, tap_sum(col[8:12], psi_steps))
    for tile in range(0, tail_re_ref.shape[1], LANES):
        there = slice(tile, min(tile + LANES, tail_re_ref.shape[1]))
        size = there.stop - there.start
        first = tile // lats
        tail_re_ref[here, there] = (spread(along_re, first, lats) * across)[:, :size]
        tail_im_ref[here, there] = -(spread(along_im, first, lats) * across)[:, :size]


def coef_kernel(
    sizes,
    alm_hbm,
    beam_hbm,
    table_hbm,
    weights_hbm,
    base_hbm,
    counts_hbm,
    out_ref,
    re_ref,
    im_ref,
    tail_re_ref,
    tail_im_ref,
    alm,
    beam,
    table,
    weights,
    base,
    counts,
    mixed,
    rows,
    cols,
    sems,
):
    n_strip, n_mr = lax.axis_size("strip"), lax.axis_size("mr")
    orders, lanes, ells = table.shape
    k_count = beam.shape[0]
    lats = lanes // k_count
    k_pad = mixed.shape[1] // 2
    small = [(alm_hbm, alm), (beam_hbm, beam)]
    slot = [(weights_hbm, weights), (base_hbm, base), (counts_hbm, counts)]
    pairs = small + slot + [(table_hbm.at[m], table.at[m]) for m in range(orders)]
    copies = [
        pltpu.make_async_copy(source, target, sems.at[i])
        for i, (source, target) in enumerate(pairs)
    ]
    small, slot, big = copies[:2], copies[2:5], copies[5:]
    for copy in copies:
        copy.start()
    mixed[...] = jnp.zeros_like(mixed)

    fixed = fixed_rows(sizes, n_strip, n_mr, orders, re_ref.shape[1])
    for copy in slot:
        copy.wait()
    cols[...] = slot_rows(sizes, weights[...], base[...], counts[...], n_strip, n_mr).T
    block = cols.shape[0] // orders

    def mix(m):
        for c in range(2):
            product = alm[c, m, :].astype(jnp.float32)[None, :] * beam[...]
            mixed[m, c * k_pad : c * k_pad + k_count, :] = product.astype(jnp.bfloat16)

    for copy in small:
        copy.wait()
    mix(0)
    steps = [[0]] + [[m, m + 1] for m in range(1, orders - 1, 2)] + [[orders - 1]]
    for at, step in enumerate(steps):
        for m in step:
            big[m].wait()
        for m in step:
            y = lax.dot_general(mixed[m], table[m], NT, preferred_element_type=jnp.float32)
            of_row = lax.broadcasted_iota(jnp.int32, y.shape, 0) % k_pad
            of_lane = lax.broadcasted_iota(jnp.int32, y.shape, 1) // lats
            y = jnp.where(of_row == of_lane, y, 0.0)
            for c in range(2):
                total = jnp.sum(y[c * k_pad : (c + 1) * k_pad], axis=0, keepdims=True)
                rows[c * orders + m : c * orders + m + 1, :] = total
        for m in range(2 * at, min(2 * at + 2, orders)):
            here = slice(m * block, (m + 1) * block)
            slot_weights(
                sizes,
                cols[here],
                fixed,
                orders,
                (re_ref, im_ref, tail_re_ref, tail_im_ref),
                here,
            )
        for m in range(step[-1] + 1, min(step[-1] + 3, orders)):
            mix(m)
    out_ref[...] = rows[...].astype(jnp.bfloat16)


def local_part(alm, beam, wigner, base_index, interp_weights, live_counts, n_strip, n_mr):
    orders, k_count, lats, ells = wigner.shape
    k_pad = -(-k_count // 8) * 8
    lanes = k_count * lats
    slots = base_index.shape[0]
    m_total = orders * n_strip * n_mr
    width = 2 * m_total
    sizes = (2 * m_total, lats, 2 * k_count - 1, 1.0 / math.sqrt(m_total * k_count))
    base = base_index.reshape(1, slots)
    return pl.pallas_call(
        functools.partial(coef_kernel, sizes),
        out_shape=(
            jax.ShapeDtypeStruct((2 * orders, lanes), jnp.bfloat16),
            jax.ShapeDtypeStruct((slots, width), jnp.bfloat16),
            jax.ShapeDtypeStruct((slots, width), jnp.bfloat16),
            jax.ShapeDtypeStruct((slots, lanes), jnp.float32),
            jax.ShapeDtypeStruct((slots, lanes), jnp.float32),
        ),
        in_specs=[pl.BlockSpec(memory_space=pltpu.HBM)] * 6,
        out_specs=(VMEM,) * 5,
        scratch_shapes=[
            pltpu.VMEM(alm.shape, alm.dtype),
            pltpu.VMEM(beam.shape, beam.dtype),
            pltpu.VMEM((orders, lanes, ells), wigner.dtype),
            pltpu.VMEM(interp_weights.shape, interp_weights.dtype),
            pltpu.VMEM(base.shape, base.dtype),
            pltpu.VMEM(live_counts.shape, live_counts.dtype),
            pltpu.VMEM((orders, 2 * k_pad, ells), jnp.bfloat16),
            pltpu.VMEM((2 * orders, lanes), jnp.float32),
            pltpu.VMEM((slots, 16), jnp.float32),
            pltpu.SemaphoreType.DMA((orders + 5,)),
        ],
        compiler_params=pltpu.CompilerParams(vmem_limit_bytes=48 << 20),
        cost_estimate=pl.CostEstimate(
            flops=4 * wigner.size, bytes_accessed=2 * wigner.size, transcendentals=0
        ),
        name="coef",
    )(
        *(
            pltpu.with_memory_space_constraint(x, pltpu.HBM)
            for x in (
                alm,
                beam,
                wigner.reshape(orders, lanes, ells),
                interp_weights,
                base,
                live_counts,
            )
        )
    )


def sample_kernel(first, re_ref, im_ref, tail_re_ref, tail_im_ref, *refs):
    *parts, before_ref, out_ref, coef = refs
    start = 0
    for part in parts:
        coef[start : start + part.shape[0], :] = part[...]
        start += part.shape[0]
    slots, lanes = tail_re_ref.shape
    block = min(slots, 256)
    whole = lanes // LANES * LANES
    for i in range(0, slots, block):
        here = slice(i, i + block)
        both = [ref[here, first : first + start] for ref in (re_ref, im_ref)]
        both = jnp.concatenate(both, axis=0)
        both = jnp.dot(both, coef[...], preferred_element_type=jnp.float32)
        terms = both[:block] * tail_re_ref[here] + both[block:] * tail_im_ref[here]
        total = before_ref[:, here]
        if whole:
            tiles = [terms[:, j : j + LANES] for j in range(0, whole, LANES)]
            total = total + jnp.sum(sum(tiles).T, axis=0, keepdims=True)
        if whole < lanes:
            total = total + jnp.sum(terms[:, whole:].T, axis=0, keepdims=True)
        out_ref[:, here] = total


def sample(phases, first, parts, before):
    slots, lanes = phases[2].shape
    rows = sum(part.shape[0] for part in parts)
    return pl.pallas_call(
        functools.partial(sample_kernel, first),
        out_shape=jax.ShapeDtypeStruct((1, slots), jnp.float32),
        in_specs=[VMEM] * (5 + len(parts)),
        out_specs=VMEM,
        scratch_shapes=[pltpu.VMEM((rows, lanes), jnp.bfloat16)],
        compiler_params=pltpu.CompilerParams(vmem_limit_bytes=32 << 20),
        cost_estimate=pl.CostEstimate(
            flops=4 * slots * rows * lanes, bytes_accessed=1 << 20, transcendentals=0
        ),
        name="sample",
    )(*phases, *parts, before)


def on_device(alm, beam, wigner, base_index, interp_weights, live_counts):
    n_strip = lax.axis_size("strip")
    n_mr = lax.axis_size("mr")
    mine, *phases = local_part(
        alm, beam, wigner, base_index, interp_weights, live_counts, n_strip, n_mr
    )

    def swap(x, even, odd=None):
        masks = (even, even if odd is None else odd)
        pairs = [(i, i ^ masks[i % 2]) for i in range(n_strip * n_mr)]
        return lax.ppermute(x, ("strip", "mr"), pairs)

    half = n_strip // 2
    opposite = swap(mine, half * n_mr)
    pair = jnp.concatenate([mine, swap(mine, 1)], axis=0)
    column = [swap(pair, d * n_mr, (d + half) * n_mr) for d in range(1, half)]
    column = jnp.concatenate([mine, opposite] + column, axis=0)
    plane = [column] + [swap(column, mr + 1) for mr in range(n_mr - 2, 0, -2)]
    other = [swap(part, 1) for part in plane]
    parts = plane + other
    early, late = parts[:-2], parts[-2:]
    zero = jnp.zeros((1, base_index.shape[0]), jnp.float32)
    result = sample(phases, 0, early, zero)
    result = sample(phases, sum(part.shape[0] for part in early), late, result)
    return result.reshape(-1)


def solution(mesh):
    placed = (
        P(None, ("strip", "mr"), None),
        P(),
        P(("strip", "mr"), None, None, None),
        P(("strip", "mr")),
        P(None, ("strip", "mr")),
        P(("strip", "mr"), None),
    )
    return jax.shard_map(
        on_device, mesh=mesh, in_specs=placed, out_specs=P(("strip", "mr")), check_vma=False
    )
```
